32 devices in a mesh: group: 2 (over x), branch: 8 (over z, y), expert: 2 (over core).
Axes of the slice: x: 2, y: 2, z: 4, core: 2. Of those that a mesh axis runs over, the one named last changes fastest.
Arguments:
- latent_cache: bfloat16 [16, 2048, 512], P(('group', 'branch'), 'expert'), parts along dimension 0, may hold values from -4 to 4
- rope_cache: bfloat16 [16, 256, 512], P(('group', 'branch'), 'expert'), parts along dimension 0, may hold values from -4 to 4
- q_latent: bfloat16 [256, 2, 128, 512], P(('group', 'branch', 'expert')), parts along dimension 0, may hold values from -4.8 to 4.8
- q_rope: bfloat16 [256, 2, 8192], P(('group', 'branch', 'expert')), parts along dimension 0, may hold values from -192 to 192
- new_latent: bfloat16 [256, 2, 512], P(('group', 'branch', 'expert')), parts along dimension 0, may hold values from -4 to 4
- new_rope: bfloat16 [256, 2, 64], P(('group', 'branch', 'expert')), parts along dimension 0, may hold values from -4.2 to 4.2
- branch_slot: int32 [256], P(('group', 'branch', 'expert')), parts along dimension 0, may hold values from 0 to 7, as said below
- moe_input: bfloat16 [256, 2, 7168], P(('group', 'branch', 'expert')), parts along dimension 0, may hold values from -6 to 6
- routes: int32 [256, 2, 8], P(('group', 'branch', 'expert')), parts along dimension 0, may hold values from 0 to 255, as said below
- route_gate: float32 [256, 2, 8], P(('group', 'branch', 'expert')), parts along dimension 0, may hold values from 0.05 to 0.6
- w_gate: bfloat16 [16, 7168, 128], P(('branch', 'expert')), may hold values from -0.0625 to 0.0625
- w_up: bfloat16 [16, 7168, 128], P(('branch', 'expert')), may hold values from -0.0625 to 0.0625
- w_down: bfloat16 [16, 128, 7168], P(('branch', 'expert')), may hold values from -0.1875 to 0.1875
Outputs:
- attended: bfloat16 [256, 2, 128, 512], P(('group', 'branch', 'expert')), parts along dimension 0
- moe_out: bfloat16 [256, 2, 7168], P(('group', 'branch', 'expert')), parts along dimension 0
The draws below stay inside these ranges and needn't reach their ends.
There are 2 independent parts, one for each index of `group`. The reference program is written for one: setup_inputs(seed, part) draws one part's arguments, and reference() takes and returns one part's arrays. A program takes and returns all parts, laid end to end along the dimension named above; an argument that names none is the same for every part. Nothing has to cross between parts.
Inputs may be any that keep to these rules, and one draw needn't show every extreme that they name: `branch_slot`: among the 8 tokens of one device every number from 0 to 7 stands exactly once. `routes`: each row (a token at a step) names 8 different experts, at most one of them below 2; within the 16 rows of one device no expert below 2 is named more than 2 times, and some one exactly 2 times.
All inputs are finite; a program needn't handle non-finite values.
Results may differ from the reference program's by a relative error of at most 0.0057.
Values may be sent and summed in bfloat16 or wider, within the bound.
A program may use at most 192 MiB of HBM per device.

```python
import math
import jax
import jax.numpy as jnp
from jax import lax

D = 7168
HEADS = 128
LAT = 512
ROPE = 64
ALL_EXPERTS = 256
EXP_HID = 1024
SHARDS = 8
TOPK = 8
STEPS = 2
BRANCHES = 16
BLOCK = 8
LEN = 2048
OUTLINES = 8
TOKENS = 128
EXPERTS = 2
CAP = 2


def draw_branch_slot(key, part):
    devices = TOKENS // BLOCK
    scores = jax.random.randint(jax.random.fold_in(key, 11), (devices, BLOCK), 0, 1 << 20)
    scores = scores * BLOCK + jnp.arange(BLOCK, dtype=jnp.int32)[None, :]
    return jnp.argsort(scores, axis=1).astype(jnp.int32).reshape(TOKENS)


def draw_routes(key, part):
    devices = TOKENS // BLOCK
    row_count = STEPS * BLOCK
    others = ALL_EXPERTS - EXPERTS
    keys = jax.random.split(jax.random.fold_in(key, 37), 5)
    scores = jax.random.randint(keys[0], (devices, row_count, others), 0, 1 << 20)
    scores = scores * others + jnp.arange(others, dtype=jnp.int32)[None, None, :]
    unused, picks = lax.top_k(scores, TOPK)
    picks = (picks % others + EXPERTS).astype(jnp.int32)
    order_scores = jax.random.randint(keys[1], (devices, EXPERTS), 0, 1 << 20) * EXPERTS + jnp.arange(EXPERTS, dtype=jnp.int32)[None, :]
    expert_order = jnp.argsort(order_scores, axis=1).astype(jnp.int32)
    row_scores = jax.random.randint(keys[2], (devices, row_count), 0, 1 << 20) * row_count + jnp.arange(row_count, dtype=jnp.int32)[None, :]
    row_order = jnp.argsort(row_scores, axis=1).astype(jnp.int32)
    rank = jnp.argsort(row_order, axis=1).astype(jnp.int32)
    pair = rank // CAP
    kept = (pair < EXPERTS) & ((rank < CAP) | (jax.random.randint(keys[3], (devices, row_count), 0, 8) < 7))
    computed = jnp.take_along_axis(expert_order, jnp.minimum(pair, EXPERTS - 1), axis=1)
    where_slot = jax.random.randint(keys[4], (devices, row_count), 0, TOPK)
    column = jnp.arange(TOPK, dtype=jnp.int32)[None, None, :]
    replace = kept[:, :, None] & (column == where_slot[:, :, None])
    chosen = jnp.where(replace, computed[:, :, None], picks)
    return chosen.reshape(TOKENS, STEPS, TOPK).astype(jnp.int32)


def shared_draws(key, part):
    keys = jax.random.split(jax.random.fold_in(key, 23), 5)
    rope = jnp.clip(jax.random.normal(keys[0], (OUTLINES, LEN, ROPE), jnp.float32), -4.0, 4.0)
    rope_new = jnp.clip(jax.random.normal(keys[1], (TOKENS, STEPS, ROPE), jnp.float32), -4.0, 4.0)
    latent_new = jnp.clip(jax.random.normal(keys[2], (TOKENS, STEPS, LAT), jnp.float32), -4.0, 4.0)
    query_rope = jnp.clip(jax.random.normal(keys[3], (TOKENS, STEPS, HEADS, ROPE), jnp.float32), -4.0, 4.0)
    query_lat = jnp.clip(jax.random.normal(keys[4], (TOKENS, STEPS, HEADS, LAT), jnp.float32), -4.0, 4.0)
    query_lat = query_lat + 0.2 * latent_new[:, :, None, :]
    return (rope, rope_new, latent_new, query_rope, query_lat)


def draw_rope_cache(key, part):
    return shared_draws(key, part)[0].reshape(OUTLINES, LEN // 8, 8 * ROPE).astype(jnp.bfloat16)


def draw_new_rope(key, part):
    return shared_draws(key, part)[1].astype(jnp.bfloat16)


def draw_new_latent(key, part):
    return shared_draws(key, part)[2].astype(jnp.bfloat16)


def draw_q_rope(key, part):
    return shared_draws(key, part)[3].reshape(TOKENS, STEPS, HEADS * ROPE).astype(jnp.bfloat16)


def draw_q_latent(key, part):
    return shared_draws(key, part)[4].astype(jnp.bfloat16)


def steps_of(key, dims, pieces, low, largest):
    level = 1.0
    for dim, blocks in pieces:
        heights = jax.random.uniform(jax.random.fold_in(jax.random.fold_in(key, 6), dim), (blocks,), jnp.float32, low / len(pieces), largest / len(pieces))
        level = level * jnp.repeat(jnp.exp(heights), dims[dim] // blocks).reshape((-1,) + (1,) * (len(dims) - 1 - dim))
    return level


def normal_values(rng, dims, scale, limit, shards=(), held_as=jnp.bfloat16):
    gain = steps_of(rng, dims, shards, -0.22, 0.18) if shards else 1.0
    drawn = jax.random.normal(rng, dims, jnp.float32) * scale * gain
    return jnp.minimum(jnp.maximum(drawn, -limit), limit).astype(held_as)


def setup_inputs(seed: int = 0, part: int = 0) -> dict:
    key_list = jax.random.split(jax.random.key(seed), 14)
    part_splits = jax.random.split(jax.random.fold_in(key_list[13], part), 14)
    return {
        "latent_cache": normal_values(part_splits[0], (OUTLINES, LEN, LAT), 1.0, 4.0, ((0, 8), (1, 2))),
        "rope_cache": draw_rope_cache(jax.random.fold_in(jax.random.fold_in(key_list[13], part), 71), part),
        "q_latent": draw_q_latent(jax.random.fold_in(jax.random.fold_in(key_list[13], part), 71), part),
        "q_rope": draw_q_rope(jax.random.fold_in(jax.random.fold_in(key_list[13], part), 71), part),
        "new_latent": draw_new_latent(jax.random.fold_in(jax.random.fold_in(key_list[13], part), 71), part),
        "new_rope": draw_new_rope(jax.random.fold_in(jax.random.fold_in(key_list[13], part), 71), part),
        "branch_slot": draw_branch_slot(jax.random.fold_in(jax.random.fold_in(key_list[13], part), 71), part),
        "moe_input": normal_values(part_splits[7], (TOKENS, STEPS, D), 1.0, 6.0, ((0, 16),)),
        "routes": draw_routes(jax.random.fold_in(jax.random.fold_in(key_list[13], part), 71), part),
        "route_gate": jnp.clip(jnp.exp(math.log(0.6) - 2.4849067 * jax.random.uniform(part_splits[9], (TOKENS, STEPS, TOPK), jnp.float32) ** steps_of(part_splits[9], (TOKENS, STEPS, TOPK), ((0, 16),), -0.2, 0.2)), 0.05, 0.6),
        "w_gate": normal_values(key_list[10], (EXPERTS * SHARDS, D, EXP_HID // SHARDS), D ** -0.5, 0.0625, ((0, 16),)),
        "w_up": normal_values(key_list[11], (EXPERTS * SHARDS, D, EXP_HID // SHARDS), D ** -0.5, 0.0625, ((0, 16),)),
        "w_down": normal_values(key_list[12], (EXPERTS * SHARDS, EXP_HID // SHARDS, D), EXP_HID ** -0.5, 0.1875, ((0, 16),)),
    }


softmax_scale = 192.0 ** -0.5


def cache_partial(query_lat, query_rope, keys_lat, keys_rope):
    highest = lax.Precision.HIGHEST
    scores = jnp.einsum("tshc,pc->tshp", query_lat, keys_lat, precision=highest)
    scores = scores + jnp.einsum("tshr,pr->tshp", query_rope, keys_rope, precision=highest)
    scores = scores * softmax_scale
    cache_peak = jnp.max(scores, axis=-1)
    exponent = jnp.exp(scores - cache_peak[..., None])
    totals = jnp.sum(exponent, axis=-1)
    weights = lax.optimization_barrier(exponent.astype(jnp.bfloat16)).astype(jnp.float32)
    summed = jnp.einsum("tshp,pc->tshc", weights, keys_lat, precision=highest)
    return cache_peak, totals, summed


def expert_ffn(packed):
    arrived, gate_matrix, up_matrix, down_matrix = packed
    highest = lax.Precision.HIGHEST
    inputs = arrived.astype(jnp.float32)
    gate_value = jnp.einsum("rd,jdh->jrh", inputs, gate_matrix.astype(jnp.float32), precision=highest)
    lifted = jnp.einsum("rd,jdh->jrh", inputs, up_matrix.astype(jnp.float32), precision=highest)
    hidden = lax.optimization_barrier((jax.nn.silu(gate_value) * lifted).astype(jnp.bfloat16)).astype(jnp.float32)
    parts = jnp.einsum("jrh,jhd->jrd", hidden, down_matrix.astype(jnp.float32), precision=highest)
    parts = lax.optimization_barrier(parts.astype(jnp.bfloat16)).astype(jnp.float32)
    return jnp.sum(parts, axis=0)


def reference(latent_cache, rope_cache, q_latent, q_rope, new_latent, new_rope, branch_slot, moe_input, routes, route_gate, w_gate, w_up, w_down):
    highest = lax.Precision.HIGHEST
    token_ids = jnp.arange(TOKENS, dtype=jnp.int32)
    outline = (BLOCK * (token_ids // (BRANCHES * BLOCK)) + branch_slot).astype(jnp.int32)
    members = jnp.argsort(outline, stable=True).astype(jnp.int32).reshape(OUTLINES, BRANCHES)
    query_rope_all = q_rope.reshape(TOKENS, STEPS, HEADS, ROPE)
    rope_keys = rope_cache.reshape(OUTLINES, LEN, ROPE)

    def per_outline(outline_index):
        chosen = members[outline_index]
        query_lat = jnp.take(q_latent, chosen, axis=0).astype(jnp.float32)
        query_rope = jnp.take(query_rope_all, chosen, axis=0).astype(jnp.float32)
        keys_lat = latent_cache[outline_index].astype(jnp.float32)
        keys_rope = rope_keys[outline_index].astype(jnp.float32)
        return cache_partial(query_lat, query_rope, keys_lat, keys_rope)

    cache_peak, totals, summed = lax.map(per_outline, jnp.arange(OUTLINES, dtype=jnp.int32))
    position_of = jnp.zeros((TOKENS,), jnp.int32).at[members.reshape(-1)].set(token_ids)
    cache_peak = jnp.take(cache_peak.reshape((TOKENS,) + cache_peak.shape[2:]), position_of, axis=0)
    totals = jnp.take(totals.reshape((TOKENS,) + totals.shape[2:]), position_of, axis=0)
    summed = jnp.take(summed.reshape((TOKENS,) + summed.shape[2:]), position_of, axis=0)
    cache_out = lax.optimization_barrier((summed / totals[..., None]).astype(jnp.bfloat16)).astype(jnp.float32)
    cache_lse = cache_peak + jnp.log(totals)

    latent_own = new_latent.astype(jnp.float32)
    own_scores = jnp.einsum("tshc,tjc->tshj", q_latent.astype(jnp.float32), latent_own, precision=highest)
    own_scores = own_scores + jnp.einsum("tshr,tjr->tshj", query_rope_all.astype(jnp.float32), new_rope.astype(jnp.float32), precision=highest)
    own_scores = own_scores * softmax_scale
    causal = (jnp.arange(STEPS)[None, :] <= jnp.arange(STEPS)[:, None])[None, :, None, :]
    own_peak = jnp.max(jnp.where(causal, own_scores, -1e30), axis=-1)
    own_weight = jnp.where(causal, jnp.exp(own_scores - own_peak[..., None]), 0.0)
    own_total = jnp.sum(own_weight, axis=-1)
    own_sum = jnp.einsum("tshj,tjc->tshc", own_weight, latent_own, precision=highest)
    top_value = jnp.maximum(cache_lse, own_peak)
    factor = jnp.exp(cache_lse - top_value)
    own_factor = jnp.exp(own_peak - top_value)
    numerator = factor[..., None] * cache_out + own_factor[..., None] * own_sum
    denominator = factor + own_factor * own_total
    attended = (numerator / denominator[..., None]).astype(jnp.bfloat16)

    devices = TOKENS // BLOCK
    per_device = STEPS * BLOCK * TOPK
    slot_total = EXPERTS * devices * CAP
    flat_routes = routes.reshape(devices, per_device).astype(jnp.int32)
    inside = flat_routes < EXPERTS
    onehot = (flat_routes[:, :, None] == jnp.arange(EXPERTS, dtype=jnp.int32)[None, None, :]).astype(jnp.int32)
    position = jnp.sum((jnp.cumsum(onehot, axis=1) - onehot) * onehot, axis=2)
    slot_index = flat_routes * (devices * CAP) + jnp.arange(devices, dtype=jnp.int32)[:, None] * CAP + position
    slot_index = jnp.where(inside, slot_index, slot_total).reshape(-1).astype(jnp.int32)
    rows_flat = moe_input.reshape(TOKENS * STEPS, D)
    source = jnp.repeat(rows_flat, TOPK, axis=0)
    buffer = jnp.zeros((slot_total, D), jnp.bfloat16).at[slot_index].set(source, mode="drop")
    hid_block = EXP_HID // SHARDS
    outputs = lax.map(expert_ffn, (buffer.reshape(EXPERTS, devices * CAP, D),
                                   w_gate.reshape(EXPERTS, SHARDS, D, hid_block),
                                   w_up.reshape(EXPERTS, SHARDS, D, hid_block),
                                   w_down.reshape(EXPERTS, SHARDS, hid_block, D)))
    safe_index = jnp.minimum(slot_index, slot_total - 1).astype(jnp.int32)
    picked = jnp.take(outputs.reshape(-1, D), safe_index, axis=0).reshape(TOKENS * STEPS, TOPK, D)
    gate_used = jnp.where(inside.reshape(TOKENS * STEPS, TOPK), route_gate.reshape(TOKENS * STEPS, TOPK), 0.0)
    combined = jnp.sum(gate_used[:, :, None] * picked, axis=1)
    moe_out = combined.astype(jnp.bfloat16).reshape(TOKENS, STEPS, D)
    return attended, moe_out
```

```python
import jax
import jax.numpy as jnp
from jax import lax
from jax.experimental import pallas as pl
from jax.experimental.pallas import tpu as pltpu
from jax.sharding import PartitionSpec as P

SHARDS = 8
CAP = 2
HALF = 4
CHUNKS = 4
ROPE_PART = CHUNKS

softmax_scale = 192.0 ** (-0.5)

NT = (((1,), (1,)), ((), ()))
NN = (((1,), (0,)), ((), ()))


def flipped(r, x, bits):
    out = r - r % (1 << bits)
    for j in range(bits):
        out = out + (((r // (1 << j)) + (x // (1 << j))) % 2) * (1 << j)
    return out


def hits_of(routes, experts):
    found = []
    for e in range(experts):
        found.append(jnp.sum(jnp.where(routes == e, 1.0, 0.0), axis=1, keepdims=True))
    return found


def positions_of(found, row_count, lanes):
    lane = lax.broadcasted_iota(jnp.int32, (row_count, lanes), 1)
    table = jnp.zeros((row_count, lanes), jnp.float32)
    for e, hit in enumerate(found):
        table = table + jnp.where(lane == e, hit, 0.0)
    later = lax.broadcasted_iota(jnp.int32, (row_count, row_count), 0)
    sooner = lax.broadcasted_iota(jnp.int32, (row_count, row_count), 1)
    before = jnp.where(later > sooner, 1.0, 0.0).astype(jnp.bfloat16)
    return lax.dot_general(
        before, table.astype(jnp.bfloat16), NN, preferred_element_type=jnp.float32
    )


def attend_kernel(
    slot_ref,
    routes_ref,
    q_ref,
    rope_ref,
    new_lat_ref,
    new_rope_ref,
    keys_ref,
    krope_ref,
    moe_ref,
    w_gate_ref,
    w_up_ref,
    w_down_ref,
    answers,
    sums_ref,
    q_own,
    rope_own,
    new_lat,
    new_rope,
    kraw,
    moe_own,
    q_send,
    rope_send,
    new_send,
    q_in,
    rope_in,
    new_in,
    keys,
    kpack,
    kdup,
    result,
    picking,
    w_gate,
    w_up,
    w_down,
    blocks,
    cross_in,
    mixed,
    mixed_in,
    sib_mixed,
    stacked,
    part_own,
    part_out,
    part_in,
    pair_sum,
    pair_in,
    final,
    load_sem,
    local_sem,
    own_sem,
    cross_send,
    cross_recv,
    mix_send,
    mix_recv,
    mixsib_send,
    mixsib_recv,
    y_send,
    y_recv,
    pair_send,
    pair_recv,
    ret_send,
    ret_recv,
    flow_send,
    flow_recv,
    sib_send,
    sib_recv,
    query_send,
    query_recv,
    ans_send,
    ans_recv,
):
    branch = lax.axis_index("branch")
    core = lax.axis_index("expert")
    tok = q_ref.shape[0]
    rows = q_ref.shape[1]
    half_len = keys_ref.shape[0]
    packed_len = kpack.shape[2]
    lanes = kpack.shape[3]
    heads = rows // 2
    step_rows = half_len // CHUNKS
    place_in_half = (branch // 2) % 4
    inner = ((place_in_half + 1) // 2) % 2 == 1
    outer = ((place_in_half + 1) // 2) % 2 == 0

    def place(b, c):
        return {"branch": b, "expert": c}

    sibling = place(branch, 1 - core)

    def peer(x):
        return place(flipped(branch, x, 3), core)

    middle = peer(6)
    beside = peer(2)

    experts = blocks.shape[0]
    block_rows = blocks.shape[1]
    mine = branch // HALF

    def across(d):
        return (mine + d) % experts

    def far(d):
        return place(across(d) * HALF + branch % HALF, core)

    def load(i, src, dst):
        return pltpu.make_async_copy(src, dst, load_sem.at[i])

    key_load = load(0, keys_ref, keys.at[0, 0])
    krope_load = load(1, krope_ref, kraw)
    q_load = load(2, q_ref, q_own)
    rope_load = load(3, rope_ref, rope_own)
    lat_load = load(4, new_lat_ref, new_lat)
    new_load = load(5, new_rope_ref, new_rope)
    moe_load = load(6, moe_ref, moe_own)
    weight_loads = [
        load(7, w_gate_ref, w_gate),
        load(8, w_up_ref, w_up),
        load(9, w_down_ref, w_down),
    ]
    for copy in [krope_load, q_load, rope_load, lat_load, new_load, moe_load, key_load]:
        copy.start()
    new_send[...] = jnp.zeros_like(new_send)
    new_in[...] = jnp.zeros_like(new_in)
    barrier = pltpu.get_barrier_semaphore()
    for other in (
        [sibling, middle]
        + [peer(j) for j in range(1, HALF)]
        + [far(d) for d in range(1, experts)]
    ):
        pl.semaphore_signal(
            barrier, inc=1, device_id=other, device_id_type=pl.DeviceIdType.MESH
        )
    pl.semaphore_wait(barrier, HALF + experts)

    def remote(src, dst, send, recv, where):
        return pltpu.make_async_remote_copy(
            src_ref=src,
            dst_ref=dst,
            send_sem=send,
            recv_sem=recv,
            device_id=where,
            device_id_type=pl.DeviceIdType.MESH,
        )

    def piece(c):
        return pl.ds(c * step_rows, step_rows)

    flow_from = (0, 0, 1, 3)
    flow_to = (1, 2, 3, 2)
    flow_where = (beside, middle, middle, beside)

    def flow_copy(f, c):
        src = keys.at[flow_from[f], 0, piece(c)]
        if flow_from[f] == 0:
            src = keys_ref.at[piece(c)]
        return remote(
            src,
            keys.at[flow_to[f], 0, piece(c)],
            flow_send.at[f, c],
            flow_recv.at[f, c],
            flow_where[f],
        )

    def flow_rope(f):
        return remote(
            kpack.at[flow_from[f], 0],
            kpack.at[flow_to[f], 0],
            flow_send.at[f, ROPE_PART],
            flow_recv.at[f, ROPE_PART],
            flow_where[f],
        )

    def sib_copy(s, c):
        src = keys_ref.at[piece(c)] if s == 0 else keys.at[s, 0, piece(c)]
        return remote(
            src, keys.at[s, 1, piece(c)], sib_send.at[s, c], sib_recv.at[s, c], sibling
        )

    def sib_rope(s):
        return remote(
            kpack.at[s, 0],
            kpack.at[s, 1],
            sib_send.at[s, ROPE_PART],
            sib_recv.at[s, ROPE_PART],
            sibling,
        )

    def query_copies(x, at, where):
        return [
            remote(q_send.at[x], q_in.at[at], query_send.at[0, x], query_recv.at[0, at], where),
            remote(
                rope_send.at[x], rope_in.at[at], query_send.at[1, x], query_recv.at[1, at], where
            ),
            remote(new_send.at[x], new_in.at[at], query_send.at[2, x], query_recv.at[2, at], where),
        ]

    def answer_copy(i, x, where):
        return remote(result.at[i], answers.at[x], ans_send.at[i], ans_recv.at[x], where)

    def cross_copy(d):
        return remote(
            blocks.at[across(d)], cross_in.at[d], cross_send.at[d], cross_recv.at[d], far(d)
        )

    def mix_copy(j):
        return remote(mixed, mixed_in.at[j], mix_send.at[j], mix_recv.at[j], peer(j))

    def mixsib_copy(j):
        source = mixed if j == 0 else mixed_in.at[j]
        return remote(source, sib_mixed.at[j], mixsib_send.at[j], mixsib_recv.at[j], sibling)

    def y_copy(j):
        return remote(part_out.at[j], part_in.at[j], y_send.at[j], y_recv.at[j], sibling)

    def pair_copy(j):
        return remote(pair_sum.at[j], pair_in.at[j], pair_send.at[j], pair_recv.at[j], peer(j))

    def ret_copy(d):
        return remote(final.at[d], sums_ref.at[mine], ret_send.at[d], ret_recv.at[d], far(experts - d))

    own_sums = pltpu.make_async_copy(final.at[0], sums_ref.at[mine], own_sem.at[0])

    def make_blocks():
        moe_load.wait()
        row_count = routes_ref.shape[0]
        found = hits_of(routes_ref[...], experts)
        position = positions_of(found, row_count, lanes)
        lane = lax.broadcasted_iota(jnp.int32, (row_count, lanes), 1)
        placing = jnp.zeros((row_count, lanes), jnp.float32)
        for e, hit in enumerate(found):
            for k in range(block_rows):
                here = hit * jnp.where(position[:, e : e + 1] == float(k), 1.0, 0.0)
                placing = placing + jnp.where(lane == e * block_rows + k, here, 0.0)
        places = max(8, experts * block_rows)
        unit = jnp.where(
            lax.broadcasted_iota(jnp.int32, (places, lanes), 0)
            == lax.broadcasted_iota(jnp.int32, (places, lanes), 1),
            1.0,
            0.0,
        ).astype(jnp.bfloat16)
        turned = lax.dot_general(
            unit, placing.astype(jnp.bfloat16), NT, preferred_element_type=jnp.float32
        ).astype(jnp.bfloat16)
        tokens = jnp.concatenate(
            [moe_own[t].astype(jnp.float32) for t in range(tok)], axis=0
        ).astype(jnp.bfloat16)
        chosen = lax.dot_general(turned, tokens, NN, preferred_element_type=jnp.float32)
        for e in range(experts):
            blocks[e] = chosen[e * block_rows : (e + 1) * block_rows].astype(jnp.bfloat16)
        for d in range(1, experts):
            cross_copy(d).start()

    def mix_blocks():
        mixed[0] = blocks[mine]
        for d in range(1, experts):
            cross_copy(d).wait_recv()
            mixed[d] = cross_in[d]
        for j in (2, 3, 1):
            mix_copy(j).start()

    def share_blocks():
        mixsib_copy(0).start()
        for j in range(1, HALF):
            mix_copy(j).wait_recv()
            mixsib_copy(j).start()

    def feed_forward():
        for j in range(0, HALF):
            mixsib_copy(j).wait_recv()
        for copy in weight_loads:
            copy.wait()
        pieces = [mixed] + [mixed_in.at[j] for j in range(1, HALF)]
        pieces = pieces + [sib_mixed.at[j] for j in range(HALF)]
        rows_of = [p[d].astype(jnp.float32) for p in pieces for d in range(experts)]
        stacked[...] = jnp.concatenate(rows_of, axis=0).astype(jnp.bfloat16)
        gate = jnp.dot(stacked[...], w_gate[...], preferred_element_type=jnp.float32)
        lifted = jnp.dot(stacked[...], w_up[...], preferred_element_type=jnp.float32)
        hidden = (gate / (1.0 + jnp.exp(-gate)) * lifted).astype(jnp.bfloat16)
        parts = jnp.dot(hidden, w_down[...], preferred_element_type=jnp.float32)
        for j in range(HALF):
            for d in range(experts):
                own_at = (j * experts + d) * block_rows
                sib_at = own_at + HALF * experts * block_rows
                part_own[j, d] = parts[own_at : own_at + block_rows]
                part_out[j, d] = parts[sib_at : sib_at + block_rows]
            y_copy(j).start()

    def add_pairs():
        for j in (2, 3, 1, 0):
            y_copy(j).wait_recv()
            part_own[j] = part_own[j] + part_in[j]
            pair_sum[j] = part_own[j].astype(jnp.bfloat16)
            if j:
                pair_copy(j).start()

    def finish_sums():
        total = part_own[0]
        for j in range(1, HALF):
            pair_copy(j).wait_recv()
            total = total + pair_in[j].astype(jnp.float32)
        final[...] = total.astype(jnp.bfloat16)
        own_sums.start()
        for d in range(1, experts):
            ret_copy(d).start()

    def gather(x, to_q, to_rope, to_new):
        want = flipped(branch % tok, x, 3)
        at = 0
        for t in range(tok):
            at = jnp.where(slot_ref[t] == want, t, at)
        to_q[x] = q_own[at]
        to_rope[x] = rope_own[at]
        lat = new_lat.shape[2]
        fresh_rope = new_rope[at].astype(jnp.float32)
        to_new[x, 0:2, pl.ds(0, lat)] = new_lat[at]
        to_new[x, 0:2, pl.ds(lat, lanes)] = jnp.concatenate(
            [fresh_rope, fresh_rope], axis=1
        ).astype(jnp.bfloat16)

    def send_query(x, at, where):
        gather(x, q_send, rope_send, new_send)
        for copy in query_copies(x, at, where):
            copy.start()

    def await_query(at):
        for copy in query_copies(0, at, beside):
            copy.wait_recv()

    low = lax.broadcasted_iota(jnp.int32, (packed_len, lanes), 1) < lanes // 2

    def pack_rope():
        krope_load.wait()
        groups = kraw.shape[1] // lanes
        depth = kraw.shape[0] // 2
        wide = jnp.concatenate(
            [
                jnp.concatenate(
                    [
                        kraw[pl.ds(h * depth, depth), pl.ds(g * lanes, lanes)]
                        for g in range(groups)
                    ],
                    axis=0,
                )
                for h in range(2)
            ],
            axis=1,
        )
        at = lax.broadcasted_iota(jnp.int32, (packed_len, groups * depth), 0)
        of = lax.broadcasted_iota(jnp.int32, (packed_len, groups * depth), 1)
        want = (at % (2 * groups)) // 2 * depth + at // (2 * groups)
        spreading = jnp.where(of == want, 1.0, 0.0).astype(jnp.bfloat16)
        both = lax.dot_general(spreading, wide, NN, preferred_element_type=jnp.float32)
        first = both[:, :lanes]
        later = both[:, lanes:]
        even = lax.broadcasted_iota(jnp.int32, (packed_len, lanes), 0) % 2 == 0
        left = jnp.where(even, first, pltpu.roll(first, lanes // 2, 1))
        right = jnp.where(even, pltpu.roll(later, lanes // 2, 1), later)
        kpack[0, 0] = jnp.where(low, left, right).astype(jnp.bfloat16)

    def spread(s, h):
        values = kpack[s, h].astype(jnp.float32)
        turned = pltpu.roll(values, lanes // 2, 1)
        kdup[s, h, pl.ds(0, packed_len)] = jnp.where(low, values, turned).astype(jnp.bfloat16)
        kdup[s, h, pl.ds(packed_len, packed_len)] = jnp.where(low, turned, values).astype(
            jnp.bfloat16
        )

    second = lax.broadcasted_iota(jnp.int32, (rows, 1), 0) >= heads
    half_of_row = lax.broadcasted_iota(jnp.int32, (rows, lanes), 0) % 2
    half_of_lane = lax.broadcasted_iota(jnp.int32, (rows, lanes), 1) // (lanes // 2)
    same_half = half_of_row == half_of_lane

    def make_picking():
        at = lax.broadcasted_iota(jnp.int32, picking.shape, 0)
        of = lax.broadcasted_iota(jnp.int32, picking.shape, 1)
        want = 2 * ((at % heads) // 2) + at // heads
        picking[...] = jnp.where(of == want, 1.0, 0.0).astype(jnp.bfloat16)

    def attend(i, s):
        q = q_in[i]
        spaced = lax.dot_general(picking[...], rope_in[i], NN, preferred_element_type=jnp.float32)
        qr = jnp.where(same_half, spaced, 0.0).astype(jnp.bfloat16)
        fresh = new_in[i]
        lat = q.shape[1]

        def score(k, kr):
            return lax.dot_general(q, k, NT, preferred_element_type=jnp.float32) + lax.dot_general(
                qr, kr, NT, preferred_element_type=jnp.float32
            )

        own = score(fresh[:, :lat], fresh[:, lat:])
        own0 = own[:, 0:1]
        own1 = jnp.where(second, own[:, 1:2], -1e30)
        s0 = score(keys[s, 0], kdup[s, 0])
        s1 = score(keys[s, 1], kdup[s, 1])
        top = jnp.maximum(jnp.max(s0, axis=1, keepdims=True), jnp.max(s1, axis=1, keepdims=True))
        top = jnp.maximum(top, jnp.maximum(own0, own1))
        p0 = jnp.exp((s0 - top) * softmax_scale)
        p1 = jnp.exp((s1 - top) * softmax_scale)
        w0 = jnp.exp((own0 - top) * softmax_scale)
        w1 = jnp.where(second, jnp.exp((own1 - top) * softmax_scale), 0.0)
        total = jnp.sum(p0, axis=1, keepdims=True) + jnp.sum(p1, axis=1, keepdims=True) + w0 + w1
        summed = lax.dot_general(
            p0.astype(jnp.bfloat16), keys[s, 0], NN, preferred_element_type=jnp.float32
        ) + lax.dot_general(
            p1.astype(jnp.bfloat16), keys[s, 1], NN, preferred_element_type=jnp.float32
        )
        entries = fresh[:, :lat].astype(jnp.float32)
        summed = summed + w0 * entries[0:1] + w1 * entries[1:2]
        return (summed / total).astype(jnp.bfloat16)

    def local_copy(x):
        return pltpu.make_async_copy(result.at[x], answers.at[x], local_sem.at[x])

    def both_tokens(x, s, ahead):
        def body(i, carry):
            remote_turn = i if not ahead else 1 - i
            at = x + remote_turn

            @pl.when(remote_turn == 1)
            def _():
                await_query(at)

            result[at] = attend(at, s)

            @pl.when(remote_turn == 1)
            def _():
                answer_copy(at, at, peer(1)).start()

            @pl.when(remote_turn == 0)
            def _():
                local_copy(at).start()

            return carry

        lax.fori_loop(0, 2, body, 0)

    def await_sibling(s):
        for c in range(CHUNKS):
            sib_copy(s, c).wait_recv()
        sib_rope(s).wait_recv()
        spread(s, 1)

    for c in range(CHUNKS):
        sib_copy(0, c).start()
        flow_copy(0, c).start()

        @pl.when(inner)
        def _():
            flow_copy(1, c).start()

    for copy in weight_loads:
        copy.start()
    for copy in [q_load, rope_load, lat_load, new_load]:
        copy.wait()
    send_query(1, 1, peer(1))
    pack_rope()
    sib_rope(0).start()
    flow_rope(0).start()

    @pl.when(inner)
    def _():
        flow_rope(1).start()

    make_blocks()
    send_query(3, 3, peer(1))
    make_picking()
    spread(0, 0)
    gather(0, q_in, rope_in, new_in)
    key_load.wait()
    await_sibling(0)
    mix_blocks()
    send_query(7, 7, peer(1))

    @pl.when(inner)
    def _():
        send_query(5, 5, peer(1))
        gather(4, q_in, rope_in, new_in)

    @pl.when(outer)
    def _():
        send_query(4, 8, peer(2))
        send_query(5, 9, peer(3))

    for x in (2, 6):
        gather(x, q_in, rope_in, new_in)
    both_tokens(0, 0, False)
    share_blocks()

    def arrived(c):
        flow_copy(0, c).wait_recv()
        sib_copy(1, c).start()

        @pl.when(inner)
        def _():
            flow_copy(2, c).start()

    for c in range(2):
        arrived(c)
    feed_forward()
    for c in range(2, CHUNKS):
        arrived(c)
    flow_rope(0).wait_recv()
    sib_rope(1).start()

    @pl.when(inner)
    def _():
        flow_rope(2).start()

    add_pairs()
    spread(1, 0)
    await_sibling(1)
    both_tokens(2, 1, False)
    finish_sums()

    @pl.when(inner)
    def _():
        for c in range(CHUNKS):
            flow_copy(1, c).wait_recv()
            sib_copy(2, c).start()
        flow_rope(1).wait_recv()
        sib_rope(2).start()
        spread(2, 0)
        await_sibling(2)

        def pass_on(c):
            flow_copy(2, c).wait_recv()
            flow_copy(3, c).start()
            sib_copy(3, c).start()

        def body(i, carry):
            at = 6 + i

            @pl.when(i > 0)
            def _():
                await_query(at)

            result[at] = attend(at, 2)

            @pl.when(i == 0)
            def _():
                local_copy(at).start()

            @pl.when(i == 1)
            def _():
                answer_copy(at, at, peer(1)).start()

            pass_on(i)
            return carry

        lax.fori_loop(0, CHUNKS, body, 0)
        flow_rope(2).wait_recv()
        flow_rope(3).start()
        sib_rope(3).start()
        answer_copy(8, 4, peer(2)).start()
        answer_copy(9, 5, peer(3)).start()
        spread(3, 0)
        await_sibling(3)
        both_tokens(4, 3, True)

    @pl.when(outer)
    def _():
        for c in range(CHUNKS):
            flow_copy(3, c).wait_recv()
            sib_copy(2, c).start()
        flow_rope(3).wait_recv()
        sib_rope(2).start()
        spread(2, 0)
        await_sibling(2)
        both_tokens(6, 2, True)
        for x in (4, 5):
            answer_copy(x, x, peer(1)).wait_recv()
        for copy in query_copies(4, 8, peer(2)):
            copy.wait_send()
        for copy in query_copies(5, 9, peer(3)):
            copy.wait_send()

    @pl.when(inner)
    def _():
        answer_copy(5, 5, peer(1)).wait_recv()
        local_copy(4).wait()
        answer_copy(8, 4, peer(2)).wait_send()
        answer_copy(9, 5, peer(3)).wait_send()
        answer_copy(5, 5, peer(1)).wait_send()
        for copy in query_copies(5, 5, peer(1)):
            copy.wait_send()
        for f in (1, 2, 3):
            for c in range(CHUNKS):
                flow_copy(f, c).wait_send()
            flow_rope(f).wait_send()
        for c in range(CHUNKS):
            sib_copy(3, c).wait_send()
        sib_rope(3).wait_send()

    for x in (1, 3, 7):
        answer_copy(x, x, peer(1)).wait_recv()
        answer_copy(x, x, peer(1)).wait_send()
        for copy in query_copies(x, x, peer(1)):
            copy.wait_send()
    for x in (0, 2, 6):
        local_copy(x).wait()
    for c in range(CHUNKS):
        flow_copy(0, c).wait_send()
    flow_rope(0).wait_send()
    for s in range(3):
        for c in range(CHUNKS):
            sib_copy(s, c).wait_send()
        sib_rope(s).wait_send()
    for d in range(1, experts):
        ret_copy(d).wait_recv()
    own_sums.wait()
    for d in range(1, experts):
        cross_copy(d).wait_send()
        ret_copy(d).wait_send()
    for j in range(HALF):
        mixsib_copy(j).wait_send()
        y_copy(j).wait_send()
        if j:
            mix_copy(j).wait_send()
            pair_copy(j).wait_send()


def attention(slots, routes, q, rope, new_lat, new_rope, keys, krope, moe, w_gate, w_up, w_down):
    tok, rows, lat = q.shape
    half_len = keys.shape[0]
    lanes = 2 * new_rope.shape[-1]
    packed_len = half_len // 2
    width = moe.shape[-1]
    experts = lax.axis_size("branch") * lax.axis_size("expert") // SHARDS
    bf = jnp.bfloat16
    vmem = pl.BlockSpec(memory_space=pltpu.VMEM)
    smem = pl.BlockSpec(memory_space=pltpu.SMEM)
    anywhere = pl.BlockSpec(memory_space=pl.ANY)
    dma = pltpu.SemaphoreType.DMA
    quad = pltpu.VMEM((HALF, experts, CAP, width), bf)
    quad_sum = pltpu.VMEM((HALF, experts, CAP, width), jnp.float32)
    block = pltpu.VMEM((experts, CAP, width), bf)
    landing = tok + 2
    return pl.pallas_call(
        attend_kernel,
        out_shape=(
            jax.ShapeDtypeStruct(q.shape, bf),
            jax.ShapeDtypeStruct((experts, CAP, width), bf),
        ),
        in_specs=[smem, vmem] + [anywhere] * 10,
        out_specs=(anywhere, anywhere),
        scratch_shapes=[
            pltpu.VMEM(q.shape, bf),
            pltpu.VMEM(rope.shape, bf),
            pltpu.VMEM(new_lat.shape, bf),
            pltpu.VMEM(new_rope.shape, bf),
            pltpu.VMEM(krope.shape, bf),
            pltpu.VMEM(moe.shape, bf),
            pltpu.VMEM(q.shape, bf),
            pltpu.VMEM(rope.shape, bf),
            pltpu.VMEM((tok, 8, lat + lanes), bf),
            pltpu.VMEM((landing,) + q.shape[1:], bf),
            pltpu.VMEM((landing,) + rope.shape[1:], bf),
            pltpu.VMEM((landing, 8, lat + lanes), bf),
            pltpu.VMEM((4, 2, half_len, lat), bf),
            pltpu.VMEM((4, 2, packed_len, lanes), bf),
            pltpu.VMEM((4, 2, half_len, lanes), bf),
            pltpu.VMEM((landing,) + q.shape[1:], bf),
            pltpu.VMEM((rows, rope.shape[1]), bf),
            pltpu.VMEM(w_gate.shape, bf),
            pltpu.VMEM(w_up.shape, bf),
            pltpu.VMEM(w_down.shape, bf),
            block,
            block,
            block,
            quad,
            quad,
            pltpu.VMEM((2 * HALF * experts * CAP, width), bf),
            quad_sum,
            quad_sum,
            quad_sum,
            quad,
            quad,
            block,
            dma((10,)),
            dma((tok,)),
            dma((1,)),
            dma((experts,)),
            dma((experts,)),
            dma((HALF,)),
            dma((HALF,)),
            dma((HALF,)),
            dma((HALF,)),
            dma((HALF,)),
            dma((HALF,)),
            dma((HALF,)),
            dma((HALF,)),
            dma((experts,)),
            dma((experts,)),
            dma((4, CHUNKS + 1)),
            dma((4, CHUNKS + 1)),
            dma((4, CHUNKS + 1)),
            dma((4, CHUNKS + 1)),
            dma((3, tok)),
            dma((3, landing)),
            dma((landing,)),
            dma((tok,)),
        ],
        compiler_params=pltpu.CompilerParams(
            collective_id=0, has_side_effects=True, vmem_limit_bytes=58 * 1024 * 1024
        ),
    )(slots, routes, q, rope, new_lat, new_rope, keys, krope, moe, w_gate, w_up, w_down)


def finish_kernel(slot_ref, routes_ref, gates_ref, sums_ref, source, out, moe_out, sem):
    tok = source.shape[0]
    own = lax.axis_index("branch") % tok

    def chosen(t):
        at = 0
        for x in range(tok):
            at = jnp.where(slot_ref[t] == flipped(own, x, 3), x, at)
        return at

    def moving(t):
        return pltpu.make_async_copy(source.at[chosen(t)], out.at[t], sem.at[t])

    for t in range(tok):
        moving(t).start()
    experts, slots, width = sums_ref.shape
    routes = routes_ref[...]
    gates = gates_ref[...]
    row_count = routes.shape[0]
    found = hits_of(routes, experts)
    position = positions_of(found, row_count, 128)
    total = jnp.zeros((row_count, width), jnp.float32)
    for e, hit in enumerate(found):
        gate = jnp.sum(jnp.where(routes == e, gates, 0.0), axis=1, keepdims=True)
        rows = sums_ref[e].astype(jnp.float32)
        for k in range(slots):
            here = gate * jnp.where(position[:, e : e + 1] == float(k), 1.0, 0.0)
            total = total + here * rows[k : k + 1]
    for t in range(tok):
        steps = row_count // tok
        moe_out[t] = total[t * steps : (t + 1) * steps].astype(jnp.bfloat16)
    for t in range(tok):
        moving(t).wait()


def finished(slots, routes, gates, sums, source, moe_shape):
    anywhere = pl.BlockSpec(memory_space=pl.ANY)
    vmem = pl.BlockSpec(memory_space=pltpu.VMEM)
    tok = source.shape[0]
    return pl.pallas_call(
        finish_kernel,
        out_shape=(
            jax.ShapeDtypeStruct(source.shape, source.dtype),
            jax.ShapeDtypeStruct(moe_shape, jnp.bfloat16),
        ),
        in_specs=[pl.BlockSpec(memory_space=pltpu.SMEM), vmem, vmem, vmem, anywhere],
        out_specs=(anywhere, vmem),
        scratch_shapes=[pltpu.SemaphoreType.DMA((tok,))],
    )(slots, routes, gates, sums, source)


def on_device(
    latent_cache,
    rope_cache,
    q_latent,
    q_rope,
    new_latent,
    new_rope,
    branch_slot,
    moe_input,
    routes,
    route_gate,
    w_gate,
    w_up,
    w_down,
):
    tok_rows, step_count, head_count, lat = q_latent.shape
    lanes = 2 * new_rope.shape[-1]
    pair_rows = q_rope.shape[-1] // lanes
    rope = q_rope.reshape(tok_rows, step_count, pair_rows, lanes)
    rope = rope.transpose(0, 2, 1, 3).reshape(tok_rows, step_count * pair_rows, lanes)
    flat_routes = routes.reshape(tok_rows * step_count, -1)
    flat_gates = route_gate.reshape(tok_rows * step_count, -1)
    answers, sums = attention(
        branch_slot,
        flat_routes,
        q_latent.reshape(tok_rows, step_count * head_count, lat),
        rope,
        new_latent,
        new_rope,
        latent_cache[0],
        rope_cache[0],
        moe_input,
        w_gate[0],
        w_up[0],
        w_down[0],
    )
    attended, moe_out = finished(
        branch_slot, flat_routes, flat_gates, sums, answers, moe_input.shape
    )
    return (attended.reshape(q_latent.shape), moe_out)


def solution(mesh):
    return jax.shard_map(
        on_device,
        mesh=mesh,
        in_specs=(
            P(("group", "branch"), "expert", None),
            P(("group", "branch"), "expert", None),
            P(("group", "branch", "expert"), None, None, None),
            P(("group", "branch", "expert"), None, None),
            P(("group", "branch", "expert"), None, None),
            P(("group", "branch", "expert"), None, None),
            P(("group", "branch", "expert")),
            P(("group", "branch", "expert"), None, None),
            P(("group", "branch", "expert"), None, None),
            P(("group", "branch", "expert"), None, None),
            P(("branch", "expert"), None, None),
            P(("branch", "expert"), None, None),
            P(("branch", "expert"), None, None),
        ),
        out_specs=(
            P(("group", "branch", "expert"), None, None, None),
            P(("group", "branch", "expert"), None, None),
        ),
        check_vma=False,
    )
```

```python
import jax
import jax.numpy as jnp
from jax import lax
from jax.experimental import pallas as pl
from jax.experimental.pallas import tpu as pltpu
from jax.sharding import PartitionSpec as P

SHARDS = 8
CAP = 2
HALF = 4
CHUNKS = 8
ROPE_PART = CHUNKS

softmax_scale = 192.0 ** (-0.5)

NT = (((1,), (1,)), ((), ()))
NN = (((1,), (0,)), ((), ()))


def flipped(r, x, bits):
    out = r - r % (1 << bits)
    for j in range(bits):
        out = out + (((r // (1 << j)) + (x // (1 << j))) % 2) * (1 << j)
    return out


def hits_of(routes, experts):
    found = []
    for e in range(experts):
        found.append(jnp.sum(jnp.where(routes == e, 1.0, 0.0), axis=1, keepdims=True))
    return found


def positions_of(found, row_count, lanes):
    lane = lax.broadcasted_iota(jnp.int32, (row_count, lanes), 1)
    table = jnp.zeros((row_count, lanes), jnp.float32)
    for e, hit in enumerate(found):
        table = table + jnp.where(lane == e, hit, 0.0)
    later = lax.broadcasted_iota(jnp.int32, (row_count, row_count), 0)
    sooner = lax.broadcasted_iota(jnp.int32, (row_count, row_count), 1)
    before = jnp.where(later > sooner, 1.0, 0.0).astype(jnp.bfloat16)
    return lax.dot_general(
        before, table.astype(jnp.bfloat16), NN, preferred_element_type=jnp.float32
    )


def attend_kernel(
    slot_ref,
    routes_ref,
    q_ref,
    rope_ref,
    new_lat_ref,
    new_rope_ref,
    keys_ref,
    krope_ref,
    moe_ref,
    w_gate_ref,
    w_up_ref,
    w_down_ref,
    answers,
    sums_ref,
    q_own,
    rope_own,
    new_lat,
    new_rope,
    kraw,
    moe_own,
    q_send,
    rope_send,
    new_send,
    q_in,
    rope_in,
    new_in,
    keys,
    kpack,
    kdup,
    result,
    picking,
    w_gate,
    w_up,
    w_down,
    blocks,
    cross_in,
    mixed,
    mixed_in,
    sib_mixed,
    stacked,
    part_own,
    part_out,
    part_in,
    pair_sum,
    pair_in,
    final,
    load_sem,
    local_sem,
    own_sem,
    cross_send,
    cross_recv,
    mix_send,
    mix_recv,
    mixsib_send,
    mixsib_recv,
    y_send,
    y_recv,
    pair_send,
    pair_recv,
    ret_send,
    ret_recv,
    flow_send,
    flow_recv,
    sib_send,
    sib_recv,
    query_send,
    query_recv,
    ans_send,
    ans_recv,
):
    branch = lax.axis_index("branch")
    core = lax.axis_index("expert")
    tok = q_ref.shape[0]
    rows = q_ref.shape[1]
    half_len = keys_ref.shape[0]
    packed_len = kpack.shape[2]
    lanes = kpack.shape[3]
    heads = rows // 2
    step_rows = half_len // CHUNKS
    place_in_half = (branch // 2) % 4
    inner = ((place_in_half + 1) // 2) % 2 == 1
    outer = ((place_in_half + 1) // 2) % 2 == 0

    def place(b, c):
        return {"branch": b, "expert": c}

    sibling = place(branch, 1 - core)

    def peer(x):
        return place(flipped(branch, x, 3), core)

    middle = peer(6)
    beside = peer(2)

    experts = blocks.shape[0]
    block_rows = blocks.shape[1]
    mine = branch // HALF

    def across(d):
        return (mine + d) % experts

    def far(d):
        return place(across(d) * HALF + branch % HALF, core)

    def load(i, src, dst):
        return pltpu.make_async_copy(src, dst, load_sem.at[i])

    key_load = load(0, keys_ref, keys.at[0, 0])
    krope_load = load(1, krope_ref, kraw)
    q_load = load(2, q_ref, q_own)
    rope_load = load(3, rope_ref, rope_own)
    lat_load = load(4, new_lat_ref, new_lat)
    new_load = load(5, new_rope_ref, new_rope)
    moe_load = load(6, moe_ref, moe_own)
    weight_loads = [
        load(7, w_gate_ref, w_gate),
        load(8, w_up_ref, w_up),
        load(9, w_down_ref, w_down),
    ]
    for copy in [krope_load, q_load, rope_load, lat_load, new_load, moe_load, key_load]:
        copy.start()
    new_send[...] = jnp.zeros_like(new_send)
    new_in[...] = jnp.zeros_like(new_in)
    barrier = pltpu.get_barrier_semaphore()
    for other in (
        [sibling, middle]
        + [peer(j) for j in range(1, HALF)]
        + [far(d) for d in range(1, experts)]
    ):
        pl.semaphore_signal(
            barrier, inc=1, device_id=other, device_id_type=pl.DeviceIdType.MESH
        )
    pl.semaphore_wait(barrier, HALF + experts)

    def remote(src, dst, send, recv, where):
        return pltpu.make_async_remote_copy(
            src_ref=src,
            dst_ref=dst,
            send_sem=send,
            recv_sem=recv,
            device_id=where,
            device_id_type=pl.DeviceIdType.MESH,
        )

    def piece(c):
        return pl.ds(c * step_rows, step_rows)

    flow_from = (0, 0, 1, 3)
    flow_to = (1, 2, 3, 2)
    flow_where = (beside, middle, middle, beside)

    def flow_copy(f, c):
        src = keys.at[flow_from[f], 0, piece(c)]
        if flow_from[f] == 0:
            src = keys_ref.at[piece(c)]
        return remote(
            src,
            keys.at[flow_to[f], 0, piece(c)],
            flow_send.at[f, c],
            flow_recv.at[f, c],
            flow_where[f],
        )

    def flow_rope(f):
        return remote(
            kpack.at[flow_from[f], 0],
            kpack.at[flow_to[f], 0],
            flow_send.at[f, ROPE_PART],
            flow_recv.at[f, ROPE_PART],
            flow_where[f],
        )

    def sib_copy(s, c):
        src = keys_ref.at[piece(c)] if s == 0 else keys.at[s, 0, piece(c)]
        return remote(
            src, keys.at[s, 1, piece(c)], sib_send.at[s, c], sib_recv.at[s, c], sibling
        )

    def sib_rope(s):
        return remote(
            kpack.at[s, 0],
            kpack.at[s, 1],
            sib_send.at[s, ROPE_PART],
            sib_recv.at[s, ROPE_PART],
            sibling,
        )

    def query_copies(x, at, where):
        return [
            remote(q_send.at[x], q_in.at[at], query_send.at[0, x], query_recv.at[0, at], where),
            remote(
                rope_send.at[x], rope_in.at[at], query_send.at[1, x], query_recv.at[1, at], where
            ),
            remote(new_send.at[x], new_in.at[at], query_send.at[2, x], query_recv.at[2, at], where),
        ]

    def answer_copy(i, x, where):
        return remote(result.at[i], answers.at[x], ans_send.at[i], ans_recv.at[x], where)

    def cross_copy(d):
        return remote(
            blocks.at[across(d)], cross_in.at[d], cross_send.at[d], cross_recv.at[d], far(d)
        )

    def mix_copy(j):
        return remote(mixed, mixed_in.at[j], mix_send.at[j], mix_recv.at[j], peer(j))

    def mixsib_copy(j):
        source = mixed if j == 0 else mixed_in.at[j]
        return remote(source, sib_mixed.at[j], mixsib_send.at[j], mixsib_recv.at[j], sibling)

    def y_copy(j):
        return remote(part_out.at[j], part_in.at[j], y_send.at[j], y_recv.at[j], sibling)

    def pair_copy(j):
        return remote(pair_sum.at[j], pair_in.at[j], pair_send.at[j], pair_recv.at[j], peer(j))

    def ret_copy(d):
        return remote(final.at[d], sums_ref.at[mine], ret_send.at[d], ret_recv.at[d], far(experts - d))

    own_sums = pltpu.make_async_copy(final.at[0], sums_ref.at[mine], own_sem.at[0])

    def make_blocks():
        moe_load.wait()
        row_count = routes_ref.shape[0]
        found = hits_of(routes_ref[...], experts)
        position = positions_of(found, row_count, lanes)
        lane = lax.broadcasted_iota(jnp.int32, (row_count, lanes), 1)
        placing = jnp.zeros((row_count, lanes), jnp.float32)
        for e, hit in enumerate(found):
            for k in range(block_rows):
                here = hit * jnp.where(position[:, e : e + 1] == float(k), 1.0, 0.0)
                placing = placing + jnp.where(lane == e * block_rows + k, here, 0.0)
        places = max(8, experts * block_rows)
        unit = jnp.where(
            lax.broadcasted_iota(jnp.int32, (places, lanes), 0)
            == lax.broadcasted_iota(jnp.int32, (places, lanes), 1),
            1.0,
            0.0,
        ).astype(jnp.bfloat16)
        turned = lax.dot_general(
            unit, placing.astype(jnp.bfloat16), NT, preferred_element_type=jnp.float32
        ).astype(jnp.bfloat16)
        tokens = jnp.concatenate(
            [moe_own[t].astype(jnp.float32) for t in range(tok)], axis=0
        ).astype(jnp.bfloat16)
        chosen = lax.dot_general(turned, tokens, NN, preferred_element_type=jnp.float32)
        for e in range(experts):
            blocks[e] = chosen[e * block_rows : (e + 1) * block_rows].astype(jnp.bfloat16)
        for d in range(1, experts):
            cross_copy(d).start()

    def mix_blocks():
        mixed[0] = blocks[mine]
        for d in range(1, experts):
            cross_copy(d).wait_recv()
            mixed[d] = cross_in[d]
        for j in (2, 3, 1):
            mix_copy(j).start()

    def share_blocks():
        mixsib_copy(0).start()
        for j in range(1, HALF):
            mix_copy(j).wait_recv()
            mixsib_copy(j).start()

    def feed_forward():
        for j in range(0, HALF):
            mixsib_copy(j).wait_recv()
        for copy in weight_loads:
            copy.wait()
        pieces = [mixed] + [mixed_in.at[j] for j in range(1, HALF)]
        pieces = pieces + [sib_mixed.at[j] for j in range(HALF)]
        rows_of = [p[d].astype(jnp.float32) for p in pieces for d in range(experts)]
        stacked[...] = jnp.concatenate(rows_of, axis=0).astype(jnp.bfloat16)
        gate = jnp.dot(stacked[...], w_gate[...], preferred_element_type=jnp.float32)
        lifted = jnp.dot(stacked[...], w_up[...], preferred_element_type=jnp.float32)
        hidden = (gate / (1.0 + jnp.exp(-gate)) * lifted).astype(jnp.bfloat16)
        parts = jnp.dot(hidden, w_down[...], preferred_element_type=jnp.float32)
        for j in range(HALF):
            for d in range(experts):
                own_at = (j * experts + d) * block_rows
                sib_at = own_at + HALF * experts * block_rows
                part_own[j, d] = parts[own_at : own_at + block_rows]
                part_out[j, d] = parts[sib_at : sib_at + block_rows]
            y_copy(j).start()

    def add_pairs():
        for j in (2, 3, 1, 0):
            y_copy(j).wait_recv()
            part_own[j] = part_own[j] + part_in[j]
            pair_sum[j] = part_own[j].astype(jnp.bfloat16)
            if j:
                pair_copy(j).start()

    def finish_sums():
        total = part_own[0]
        for j in range(1, HALF):
            pair_copy(j).wait_recv()
            total = total + pair_in[j].astype(jnp.float32)
        final[...] = total.astype(jnp.bfloat16)
        own_sums.start()
        for d in range(1, experts):
            ret_copy(d).start()

    def gather(x, to_q, to_rope, to_new):
        want = flipped(branch % tok, x, 3)
        at = 0
        for t in range(tok):
            at = jnp.where(slot_ref[t] == want, t, at)
        to_q[x] = q_own[at]
        to_rope[x] = rope_own[at]
        lat = new_lat.shape[2]
        fresh_rope = new_rope[at].astype(jnp.float32)
        to_new[x, 0:2, pl.ds(0, lat)] = new_lat[at]
        to_new[x, 0:2, pl.ds(lat, lanes)] = jnp.concatenate(
            [fresh_rope, fresh_rope], axis=1
        ).astype(jnp.bfloat16)

    def send_query(x, at, where):
        gather(x, q_send, rope_send, new_send)
        for copy in query_copies(x, at, where):
            copy.start()

    def await_query(at):
        for copy in query_copies(0, at, beside):
            copy.wait_recv()

    low = lax.broadcasted_iota(jnp.int32, (packed_len, lanes), 1) < lanes // 2

    def pack_rope():
        krope_load.wait()
        groups = kraw.shape[1] // lanes
        depth = kraw.shape[0] // 2
        wide = jnp.concatenate(
            [
                jnp.concatenate(
                    [
                        kraw[pl.ds(h * depth, depth), pl.ds(g * lanes, lanes)]
                        for g in range(groups)
                    ],
                    axis=0,
                )
                for h in range(2)
            ],
            axis=1,
        )
        at = lax.broadcasted_iota(jnp.int32, (packed_len, groups * depth), 0)
        of = lax.broadcasted_iota(jnp.int32, (packed_len, groups * depth), 1)
        want = (at % (2 * groups)) // 2 * depth + at // (2 * groups)
        spreading = jnp.where(of == want, 1.0, 0.0).astype(jnp.bfloat16)
        both = lax.dot_general(spreading, wide, NN, preferred_element_type=jnp.float32)
        first = both[:, :lanes]
        later = both[:, lanes:]
        even = lax.broadcasted_iota(jnp.int32, (packed_len, lanes), 0) % 2 == 0
        left = jnp.where(even, first, pltpu.roll(first, lanes // 2, 1))
        right = jnp.where(even, pltpu.roll(later, lanes // 2, 1), later)
        kpack[0, 0] = jnp.where(low, left, right).astype(jnp.bfloat16)

    def spread(s, h):
        values = kpack[s, h].astype(jnp.float32)
        turned = pltpu.roll(values, lanes // 2, 1)
        kdup[s, h, pl.ds(0, packed_len)] = jnp.where(low, values, turned).astype(jnp.bfloat16)
        kdup[s, h, pl.ds(packed_len, packed_len)] = jnp.where(low, turned, values).astype(
            jnp.bfloat16
        )

    second = lax.broadcasted_iota(jnp.int32, (rows, 1), 0) >= heads
    half_of_row = lax.broadcasted_iota(jnp.int32, (rows, lanes), 0) % 2
    half_of_lane = lax.broadcasted_iota(jnp.int32, (rows, lanes), 1) // (lanes // 2)
    same_half = half_of_row == half_of_lane

    def make_picking():
        at = lax.broadcasted_iota(jnp.int32, picking.shape, 0)
        of = lax.broadcasted_iota(jnp.int32, picking.shape, 1)
        want = 2 * ((at % heads) // 2) + at // heads
        picking[...] = jnp.where(of == want, 1.0, 0.0).astype(jnp.bfloat16)

    def attend(i, s):
        q = q_in[i]
        spaced = lax.dot_general(picking[...], rope_in[i], NN, preferred_element_type=jnp.float32)
        qr = jnp.where(same_half, spaced, 0.0).astype(jnp.bfloat16)
        fresh = new_in[i]
        lat = q.shape[1]

        def score(k, kr):
            return lax.dot_general(q, k, NT, preferred_element_type=jnp.float32) + lax.dot_general(
                qr, kr, NT, preferred_element_type=jnp.float32
            )

        own = score(fresh[:, :lat], fresh[:, lat:])
        own0 = own[:, 0:1]
        own1 = jnp.where(second, own[:, 1:2], -1e30)
        s0 = score(keys[s, 0], kdup[s, 0])
        s1 = score(keys[s, 1], kdup[s, 1])
        top = jnp.maximum(jnp.max(s0, axis=1, keepdims=True), jnp.max(s1, axis=1, keepdims=True))
        top = jnp.maximum(top, jnp.maximum(own0, own1))
        p0 = jnp.exp((s0 - top) * softmax_scale)
        p1 = jnp.exp((s1 - top) * softmax_scale)
        w0 = jnp.exp((own0 - top) * softmax_scale)
        w1 = jnp.where(second, jnp.exp((own1 - top) * softmax_scale), 0.0)
        total = jnp.sum(p0, axis=1, keepdims=True) + jnp.sum(p1, axis=1, keepdims=True) + w0 + w1
        summed = lax.dot_general(
            p0.astype(jnp.bfloat16), keys[s, 0], NN, preferred_element_type=jnp.float32
        ) + lax.dot_general(
            p1.astype(jnp.bfloat16), keys[s, 1], NN, preferred_element_type=jnp.float32
        )
        entries = fresh[:, :lat].astype(jnp.float32)
        summed = summed + w0 * entries[0:1] + w1 * entries[1:2]
        return (summed / total).astype(jnp.bfloat16)

    def local_copy(x):
        return pltpu.make_async_copy(result.at[x], answers.at[x], local_sem.at[x])

    def both_tokens(x, s, ahead):
        def body(i, carry):
            remote_turn = i if not ahead else 1 - i
            at = x + remote_turn

            @pl.when(remote_turn == 1)
            def _():
                await_query(at)

            result[at] = attend(at, s)

            @pl.when(remote_turn == 1)
            def _():
                answer_copy(at, at, peer(1)).start()

            @pl.when(remote_turn == 0)
            def _():
                local_copy(at).start()

            return carry

        lax.fori_loop(0, 2, body, 0)

    def await_sibling(s):
        for c in range(CHUNKS):
            sib_copy(s, c).wait_recv()
        sib_rope(s).wait_recv()
        spread(s, 1)

    def own_cache(c):
        sib_copy(0, c).start()
        flow_copy(0, c).start()

        @pl.when(inner)
        def _():
            flow_copy(1, c).start()

    own_cache(0)
    make_blocks()
    own_cache(1)
    for copy in weight_loads:
        copy.start()
    for copy in [q_load, rope_load, lat_load, new_load]:
        copy.wait()
    send_query(1, 1, peer(1))
    pack_rope()
    sib_rope(0).start()
    make_picking()
    spread(0, 0)
    gather(0, q_in, rope_in, new_in)
    mix_blocks()
    for c in range(2, CHUNKS // 2):
        own_cache(c)

    @pl.when(outer)
    def _():
        send_query(4, 8, peer(2))
        send_query(5, 9, peer(3))

    send_query(3, 3, peer(1))
    for c in range(CHUNKS // 2, CHUNKS):
        own_cache(c)
    flow_rope(0).start()

    @pl.when(inner)
    def _():
        flow_rope(1).start()

    send_query(7, 7, peer(1))

    @pl.when(inner)
    def _():
        send_query(5, 5, peer(1))
        gather(4, q_in, rope_in, new_in)

    for x in (2, 6):
        gather(x, q_in, rope_in, new_in)
    key_load.wait()
    share_blocks()
    await_sibling(0)
    both_tokens(0, 0, False)

    def arrived(c):
        flow_copy(0, c).wait_recv()
        sib_copy(1, c).start()

        @pl.when(inner)
        def _():
            flow_copy(2, c).start()

    def beside_done():
        flow_rope(0).wait_recv()
        sib_rope(1).start()

        @pl.when(inner)
        def _():
            flow_rope(2).start()

        spread(1, 0)

    feed_forward()
    for c in range(CHUNKS // 2):
        arrived(c)
    add_pairs()

    @pl.when(inner)
    def _():
        for c in range(CHUNKS):
            flow_copy(1, c).wait_recv()
            sib_copy(2, c).start()
        flow_rope(1).wait_recv()
        sib_rope(2).start()
        spread(2, 0)
        await_sibling(2)

        def body(i, carry):
            first = i < 4
            at = jnp.where(i == 0, 8, jnp.where(i == 3, 9, 5 + i))
            at = jnp.where(first, at, i - 3)

            @pl.when(i < 4)
            def _():
                arrived(CHUNKS // 2 + i)

            @pl.when(i == 4)
            def _():
                beside_done()

            @pl.when(i == 5)
            def _():
                await_sibling(1)

            @pl.when((i < 4) | (i == 5) | (i == 6))
            def _():
                @pl.when((i != 1) & (i != 5))
                def _():
                    await_query(at)

                result[at] = attend(at, jnp.where(first, 2, 1))

                @pl.when(i == 0)
                def _():
                    answer_copy(8, 4, peer(2)).start()

                @pl.when((i == 1) | (i == 5))
                def _():
                    local_copy(at).start()

                @pl.when((i == 2) | (i == 6))
                def _():
                    answer_copy(at, at, peer(1)).start()

            flow_copy(2, i).wait_recv()
            flow_copy(3, i).start()
            sib_copy(3, i).start()

            @pl.when(i == 4)
            def _():
                finish_sums()

            return carry

        lax.fori_loop(0, CHUNKS, body, 0)
        flow_rope(2).wait_recv()
        flow_rope(3).start()
        sib_rope(3).start()
        answer_copy(9, 5, peer(3)).start()
        spread(3, 0)
        await_sibling(3)
        both_tokens(4, 3, True)

    @pl.when(outer)
    def _():
        for c in range(CHUNKS // 2, CHUNKS):
            arrived(c)
        beside_done()
        await_sibling(1)
        both_tokens(2, 1, False)
        finish_sums()
        for c in range(CHUNKS):
            flow_copy(3, c).wait_recv()
            sib_copy(2, c).start()
        flow_rope(3).wait_recv()
        sib_rope(2).start()
        spread(2, 0)
        await_sibling(2)
        both_tokens(6, 2, True)
        for x in (4, 5):
            answer_copy(x, x, peer(1)).wait_recv()
        for copy in query_copies(4, 8, peer(2)):
            copy.wait_send()
        for copy in query_copies(5, 9, peer(3)):
            copy.wait_send()

    @pl.when(inner)
    def _():
        answer_copy(5, 5, peer(1)).wait_recv()
        local_copy(4).wait()
        answer_copy(8, 4, peer(2)).wait_send()
        answer_copy(9, 5, peer(3)).wait_send()
        answer_copy(5, 5, peer(1)).wait_send()
        for copy in query_copies(5, 5, peer(1)):
            copy.wait_send()
        for f in (1, 2, 3):
            for c in range(CHUNKS):
                flow_copy(f, c).wait_send()
            flow_rope(f).wait_send()
        for c in range(CHUNKS):
            sib_copy(3, c).wait_send()
        sib_rope(3).wait_send()

    for x in (1, 3, 7):
        answer_copy(x, x, peer(1)).wait_recv()
        answer_copy(x, x, peer(1)).wait_send()
        for copy in query_copies(x, x, peer(1)):
            copy.wait_send()
    for x in (0, 2, 6):
        local_copy(x).wait()
    for c in range(CHUNKS):
        flow_copy(0, c).wait_send()
    flow_rope(0).wait_send()
    for s in range(3):
        for c in range(CHUNKS):
            sib_copy(s, c).wait_send()
        sib_rope(s).wait_send()
    for d in range(1, experts):
        ret_copy(d).wait_recv()
    own_sums.wait()
    for d in range(1, experts):
        cross_copy(d).wait_send()
        ret_copy(d).wait_send()
    for j in range(HALF):
        mixsib_copy(j).wait_send()
        y_copy(j).wait_send()
        if j:
            mix_copy(j).wait_send()
            pair_copy(j).wait_send()


def attention(slots, routes, q, rope, new_lat, new_rope, keys, krope, moe, w_gate, w_up, w_down):
    tok, rows, lat = q.shape
    half_len = keys.shape[0]
    lanes = 2 * new_rope.shape[-1]
    packed_len = half_len // 2
    width = moe.shape[-1]
    experts = lax.axis_size("branch") * lax.axis_size("expert") // SHARDS
    bf = jnp.bfloat16
    vmem = pl.BlockSpec(memory_space=pltpu.VMEM)
    smem = pl.BlockSpec(memory_space=pltpu.SMEM)
    anywhere = pl.BlockSpec(memory_space=pl.ANY)
    dma = pltpu.SemaphoreType.DMA
    quad = pltpu.VMEM((HALF, experts, CAP, width), bf)
    quad_sum = pltpu.VMEM((HALF, experts, CAP, width), jnp.float32)
    block = pltpu.VMEM((experts, CAP, width), bf)
    landing = tok + 2
    return pl.pallas_call(
        attend_kernel,
        out_shape=(
            jax.ShapeDtypeStruct(q.shape, bf),
            jax.ShapeDtypeStruct((experts, CAP, width), bf),
        ),
        in_specs=[smem, vmem] + [anywhere] * 10,
        out_specs=(anywhere, anywhere),
        scratch_shapes=[
            pltpu.VMEM(q.shape, bf),
            pltpu.VMEM(rope.shape, bf),
            pltpu.VMEM(new_lat.shape, bf),
            pltpu.VMEM(new_rope.shape, bf),
            pltpu.VMEM(krope.shape, bf),
            pltpu.VMEM(moe.shape, bf),
            pltpu.VMEM(q.shape, bf),
            pltpu.VMEM(rope.shape, bf),
            pltpu.VMEM((tok, 8, lat + lanes), bf),
            pltpu.VMEM((landing,) + q.shape[1:], bf),
            pltpu.VMEM((landing,) + rope.shape[1:], bf),
            pltpu.VMEM((landing, 8, lat + lanes), bf),
            pltpu.VMEM((4, 2, half_len, lat), bf),
            pltpu.VMEM((4, 2, packed_len, lanes), bf),
            pltpu.VMEM((4, 2, half_len, lanes), bf),
            pltpu.VMEM((landing,) + q.shape[1:], bf),
            pltpu.VMEM((rows, rope.shape[1]), bf),
            pltpu.VMEM(w_gate.shape, bf),
            pltpu.VMEM(w_up.shape, bf),
            pltpu.VMEM(w_down.shape, bf),
            block,
            block,
            block,
            quad,
            quad,
            pltpu.VMEM((2 * HALF * experts * CAP, width), bf),
            quad_sum,
            quad_sum,
            quad_sum,
            quad,
            quad,
            block,
            dma((10,)),
            dma((tok,)),
            dma((1,)),
            dma((experts,)),
            dma((experts,)),
            dma((HALF,)),
            dma((HALF,)),
            dma((HALF,)),
            dma((HALF,)),
            dma((HALF,)),
            dma((HALF,)),
            dma((HALF,)),
            dma((HALF,)),
            dma((experts,)),
            dma((experts,)),
            dma((4, CHUNKS + 1)),
            dma((4, CHUNKS + 1)),
            dma((4, CHUNKS + 1)),
            dma((4, CHUNKS + 1)),
            dma((3, tok)),
            dma((3, landing)),
            dma((landing,)),
            dma((tok,)),
        ],
        compiler_params=pltpu.CompilerParams(
            collective_id=0, has_side_effects=True, vmem_limit_bytes=58 * 1024 * 1024
        ),
    )(slots, routes, q, rope, new_lat, new_rope, keys, krope, moe, w_gate, w_up, w_down)


def finish_kernel(
    slot_ref, routes_ref, gates_ref, sums_ref, source, out, moe_out, held, read, write
):
    tok = source.shape[0]
    own = lax.axis_index("branch") % tok

    def chosen(t):
        at = 0
        for x in range(tok):
            at = jnp.where(slot_ref[t] == flipped(own, x, 3), x, at)
        return at

    def reading(t):
        return pltpu.make_async_copy(source.at[chosen(t)], held.at[t], read.at[t])

    def writing(t):
        return pltpu.make_async_copy(held.at[t], out.at[t], write.at[t])

    for t in range(tok):
        reading(t).start()
    experts, slots, width = sums_ref.shape
    routes = routes_ref[...]
    gates = gates_ref[...]
    row_count = routes.shape[0]
    found = hits_of(routes, experts)
    position = positions_of(found, row_count, 128)
    total = jnp.zeros((row_count, width), jnp.float32)
    for e, hit in enumerate(found):
        gate = jnp.sum(jnp.where(routes == e, gates, 0.0), axis=1, keepdims=True)
        rows = sums_ref[e].astype(jnp.float32)
        for k in range(slots):
            here = gate * jnp.where(position[:, e : e + 1] == float(k), 1.0, 0.0)
            total = total + here * rows[k : k + 1]
    for t in range(tok):
        reading(t).wait()
        writing(t).start()
    for t in range(tok):
        steps = row_count // tok
        moe_out[t] = total[t * steps : (t + 1) * steps].astype(jnp.bfloat16)
    for t in range(tok):
        writing(t).wait()


def finished(slots, routes, gates, sums, source, moe_shape):
    anywhere = pl.BlockSpec(memory_space=pl.ANY)
    vmem = pl.BlockSpec(memory_space=pltpu.VMEM)
    tok = source.shape[0]
    return pl.pallas_call(
        finish_kernel,
        out_shape=(
            jax.ShapeDtypeStruct(source.shape, source.dtype),
            jax.ShapeDtypeStruct(moe_shape, jnp.bfloat16),
        ),
        in_specs=[pl.BlockSpec(memory_space=pltpu.SMEM), vmem, vmem, vmem, anywhere],
        out_specs=(anywhere, vmem),
        scratch_shapes=[
            pltpu.VMEM(source.shape, source.dtype),
            pltpu.SemaphoreType.DMA((tok,)),
            pltpu.SemaphoreType.DMA((tok,)),
        ],
    )(slots, routes, gates, sums, source)


def on_device(
    latent_cache,
    rope_cache,
    q_latent,
    q_rope,
    new_latent,
    new_rope,
    branch_slot,
    moe_input,
    routes,
    route_gate,
    w_gate,
    w_up,
    w_down,
):
    tok_rows, step_count, head_count, lat = q_latent.shape
    lanes = 2 * new_rope.shape[-1]
    pair_rows = q_rope.shape[-1] // lanes
    rope = q_rope.reshape(tok_rows, step_count, pair_rows, lanes)
    rope = rope.transpose(0, 2, 1, 3).reshape(tok_rows, step_count * pair_rows, lanes)
    flat_routes = routes.reshape(tok_rows * step_count, -1)
    flat_gates = route_gate.reshape(tok_rows * step_count, -1)
    answers, sums = attention(
        branch_slot,
        flat_routes,
        q_latent.reshape(tok_rows, step_count * head_count, lat),
        rope,
        new_latent,
        new_rope,
        latent_cache[0],
        rope_cache[0],
        moe_input,
        w_gate[0],
        w_up[0],
        w_down[0],
    )
    attended, moe_out = finished(
        branch_slot, flat_routes, flat_gates, sums, answers, moe_input.shape
    )
    return (attended.reshape(q_latent.shape), moe_out)


def solution(mesh):
    return jax.shard_map(
        on_device,
        mesh=mesh,
        in_specs=(
            P(("group", "branch"), "expert", None),
            P(("group", "branch"), "expert", None),
            P(("group", "branch", "expert"), None, None, None),
            P(("group", "branch", "expert"), None, None),
            P(("group", "branch", "expert"), None, None),
            P(("group", "branch", "expert"), None, None),
            P(("group", "branch", "expert")),
            P(("group", "branch", "expert"), None, None),
            P(("group", "branch", "expert"), None, None),
            P(("group", "branch", "expert"), None, None),
            P(("branch", "expert"), None, None),
            P(("branch", "expert"), None, None),
            P(("branch", "expert"), None, None),
        ),
        out_specs=(
            P(("group", "branch", "expert"), None, None, None),
            P(("group", "branch", "expert"), None, None),
        ),
        check_vma=False,
    )
```

```python
import jax
import jax.numpy as jnp
from jax import lax
from jax.experimental import pallas as pl
from jax.experimental.pallas import tpu as pltpu
from jax.sharding import PartitionSpec as P

SHARDS = 8
CAP = 2
HALF = 4
CHUNKS = 8
ROPE_PART = CHUNKS

softmax_scale = 192.0 ** (-0.5)

NT = (((1,), (1,)), ((), ()))
NN = (((1,), (0,)), ((), ()))


def flipped(r, x, bits):
    out = r - r % (1 << bits)
    for j in range(bits):
        out = out + (((r // (1 << j)) + (x // (1 << j))) % 2) * (1 << j)
    return out


def hits_of(routes, experts):
    found = []
    for e in range(experts):
        found.append(jnp.sum(jnp.where(routes == e, 1.0, 0.0), axis=1, keepdims=True))
    return found


def positions_of(found, row_count, lanes):
    lane = lax.broadcasted_iota(jnp.int32, (row_count, lanes), 1)
    table = jnp.zeros((row_count, lanes), jnp.float32)
    for e, hit in enumerate(found):
        table = table + jnp.where(lane == e, hit, 0.0)
    later = lax.broadcasted_iota(jnp.int32, (row_count, row_count), 0)
    sooner = lax.broadcasted_iota(jnp.int32, (row_count, row_count), 1)
    before = jnp.where(later > sooner, 1.0, 0.0).astype(jnp.bfloat16)
    return lax.dot_general(
        before, table.astype(jnp.bfloat16), NN, preferred_element_type=jnp.float32
    )


def attend_kernel(
    slot_ref,
    routes_ref,
    q_ref,
    rope_ref,
    new_lat_ref,
    new_rope_ref,
    keys_ref,
    krope_ref,
    moe_ref,
    w_gate_ref,
    w_up_ref,
    w_down_ref,
    answers,
    sums_ref,
    q_own,
    rope_own,
    new_lat,
    new_rope,
    kraw,
    moe_own,
    q_send,
    rope_send,
    new_send,
    q_in,
    rope_in,
    new_in,
    keys,
    kpack,
    kdup,
    result,
    picking,
    w_gate,
    w_up,
    w_down,
    blocks,
    cross_in,
    mixed,
    mixed_in,
    sib_mixed,
    stacked,
    part_own,
    part_out,
    part_in,
    pair_sum,
    pair_in,
    final,
    load_sem,
    local_sem,
    own_sem,
    cross_send,
    cross_recv,
    mix_send,
    mix_recv,
    mixsib_send,
    mixsib_recv,
    y_send,
    y_recv,
    pair_send,
    pair_recv,
    ret_send,
    ret_recv,
    flow_send,
    flow_recv,
    sib_send,
    sib_recv,
    query_send,
    query_recv,
    ans_send,
    ans_recv,
):
    branch = lax.axis_index("branch")
    core = lax.axis_index("expert")
    tok = q_ref.shape[0]
    rows = q_ref.shape[1]
    half_len = keys_ref.shape[0]
    packed_len = kpack.shape[2]
    lanes = kpack.shape[3]
    heads = rows // 2
    step_rows = half_len // CHUNKS
    place_in_half = (branch // 2) % 4
    inner = ((place_in_half + 1) // 2) % 2 == 1
    outer = ((place_in_half + 1) // 2) % 2 == 0

    def place(b, c):
        return {"branch": b, "expert": c}

    sibling = place(branch, 1 - core)

    def peer(x):
        return place(flipped(branch, x, 3), core)

    middle = peer(6)
    beside = peer(2)

    experts = blocks.shape[0]
    block_rows = blocks.shape[1]
    mine = branch // HALF

    def across(d):
        return (mine + d) % experts

    def far(d):
        return place(across(d) * HALF + branch % HALF, core)

    def load(i, src, dst):
        return pltpu.make_async_copy(src, dst, load_sem.at[i])

    key_load = load(0, keys_ref, keys.at[0, 0])
    krope_load = load(1, krope_ref, kraw)
    q_load = load(2, q_ref, q_own)
    rope_load = load(3, rope_ref, rope_own)
    lat_load = load(4, new_lat_ref, new_lat)
    new_load = load(5, new_rope_ref, new_rope)
    moe_load = load(6, moe_ref, moe_own)
    weight_loads = [
        load(7, w_gate_ref, w_gate),
        load(8, w_up_ref, w_up),
        load(9, w_down_ref, w_down),
    ]
    for copy in [krope_load, q_load, rope_load, lat_load, new_load, moe_load, key_load]:
        copy.start()
    new_send[...] = jnp.zeros_like(new_send)
    new_in[...] = jnp.zeros_like(new_in)
    barrier = pltpu.get_barrier_semaphore()
    for other in (
        [sibling, middle]
        + [peer(j) for j in range(1, HALF)]
        + [far(d) for d in range(1, experts)]
    ):
        pl.semaphore_signal(
            barrier, inc=1, device_id=other, device_id_type=pl.DeviceIdType.MESH
        )
    pl.semaphore_wait(barrier, HALF + experts)

    def remote(src, dst, send, recv, where):
        return pltpu.make_async_remote_copy(
            src_ref=src,
            dst_ref=dst,
            send_sem=send,
            recv_sem=recv,
            device_id=where,
            device_id_type=pl.DeviceIdType.MESH,
        )

    def piece(c):
        return pl.ds(c * step_rows, step_rows)

    flow_from = (0, 0, 1, 3)
    flow_to = (1, 2, 3, 2)
    flow_where = (beside, middle, middle, beside)

    def flow_copy(f, c):
        src = keys.at[flow_from[f], 0, piece(c)]
        if flow_from[f] == 0:
            src = keys_ref.at[piece(c)]
        return remote(
            src,
            keys.at[flow_to[f], 0, piece(c)],
            flow_send.at[f, c],
            flow_recv.at[f, c],
            flow_where[f],
        )

    def flow_rope(f):
        return remote(
            kpack.at[flow_from[f], 0],
            kpack.at[flow_to[f], 0],
            flow_send.at[f, ROPE_PART],
            flow_recv.at[f, ROPE_PART],
            flow_where[f],
        )

    def sib_copy(s, c):
        src = keys_ref.at[piece(c)] if s == 0 else keys.at[s, 0, piece(c)]
        return remote(
            src, keys.at[s, 1, piece(c)], sib_send.at[s, c], sib_recv.at[s, c], sibling
        )

    def sib_rope(s):
        return remote(
            kpack.at[s, 0],
            kpack.at[s, 1],
            sib_send.at[s, ROPE_PART],
            sib_recv.at[s, ROPE_PART],
            sibling,
        )

    def query_copies(x, at, where):
        return [
            remote(q_send.at[x], q_in.at[at], query_send.at[0, x], query_recv.at[0, at], where),
            remote(
                rope_send.at[x], rope_in.at[at], query_send.at[1, x], query_recv.at[1, at], where
            ),
            remote(new_send.at[x], new_in.at[at], query_send.at[2, x], query_recv.at[2, at], where),
        ]

    def answer_copy(i, x, where):
        return remote(result.at[i], answers.at[x], ans_send.at[i], ans_recv.at[x], where)

    def cross_copy(d):
        return remote(
            blocks.at[across(d)], cross_in.at[d], cross_send.at[d], cross_recv.at[d], far(d)
        )

    def mix_copy(j):
        source = mixed_in.at[2] if j == 3 else mixed
        where = peer(2) if j == 2 else peer(1)
        return remote(source, mixed_in.at[j], mix_send.at[j], mix_recv.at[j], where)

    def mixsib_copy(j):
        source = mixed if j == 0 else mixed_in.at[j]
        return remote(source, sib_mixed.at[j], mixsib_send.at[j], mixsib_recv.at[j], sibling)

    def y_copy(j):
        return remote(part_out.at[j], part_in.at[j], y_send.at[j], y_recv.at[j], sibling)

    def pair_copy(j):
        where = peer(2) if j == 2 else peer(1)
        return remote(pair_sum.at[j], pair_in.at[j], pair_send.at[j], pair_recv.at[j], where)

    def ret_copy(d):
        return remote(final.at[d], sums_ref.at[mine], ret_send.at[d], ret_recv.at[d], far(experts - d))

    own_sums = pltpu.make_async_copy(final.at[0], sums_ref.at[mine], own_sem.at[0])

    def make_blocks():
        moe_load.wait()
        row_count = routes_ref.shape[0]
        found = hits_of(routes_ref[...], experts)
        position = positions_of(found, row_count, lanes)
        lane = lax.broadcasted_iota(jnp.int32, (row_count, lanes), 1)
        placing = jnp.zeros((row_count, lanes), jnp.float32)
        for e, hit in enumerate(found):
            for k in range(block_rows):
                here = hit * jnp.where(position[:, e : e + 1] == float(k), 1.0, 0.0)
                placing = placing + jnp.where(lane == e * block_rows + k, here, 0.0)
        places = max(8, experts * block_rows)
        unit = jnp.where(
            lax.broadcasted_iota(jnp.int32, (places, lanes), 0)
            == lax.broadcasted_iota(jnp.int32, (places, lanes), 1),
            1.0,
            0.0,
        ).astype(jnp.bfloat16)
        turned = lax.dot_general(
            unit, placing.astype(jnp.bfloat16), NT, preferred_element_type=jnp.float32
        ).astype(jnp.bfloat16)
        tokens = jnp.concatenate(
            [moe_own[t].astype(jnp.float32) for t in range(tok)], axis=0
        ).astype(jnp.bfloat16)
        chosen = lax.dot_general(turned, tokens, NN, preferred_element_type=jnp.float32)
        for e in range(experts):
            blocks[e] = chosen[e * block_rows : (e + 1) * block_rows].astype(jnp.bfloat16)
        for d in range(1, experts):
            cross_copy(d).start()

    def mix_blocks():
        mixed[0] = blocks[mine]
        for d in range(1, experts):
            cross_copy(d).wait_recv()
            mixed[d] = cross_in[d]
        for j in (2, 1):
            mix_copy(j).start()

    def pass_blocks():
        mixsib_copy(0).start()
        mix_copy(2).wait_recv()
        mix_copy(3).start()
        mixsib_copy(2).start()

    def share_blocks():
        for j in (1, 3):
            mix_copy(j).wait_recv()
            mixsib_copy(j).start()

    def feed_forward():
        for j in range(0, HALF):
            mixsib_copy(j).wait_recv()
        for copy in weight_loads:
            copy.wait()
        pieces = [mixed] + [mixed_in.at[j] for j in range(1, HALF)]
        pieces = pieces + [sib_mixed.at[j] for j in range(HALF)]
        rows_of = [p[d].astype(jnp.float32) for p in pieces for d in range(experts)]
        stacked[...] = jnp.concatenate(rows_of, axis=0).astype(jnp.bfloat16)
        gate = jnp.dot(stacked[...], w_gate[...], preferred_element_type=jnp.float32)
        lifted = jnp.dot(stacked[...], w_up[...], preferred_element_type=jnp.float32)
        hidden = (gate / (1.0 + jnp.exp(-gate)) * lifted).astype(jnp.bfloat16)
        parts = jnp.dot(hidden, w_down[...], preferred_element_type=jnp.float32)
        for j in range(HALF):
            for d in range(experts):
                own_at = (j * experts + d) * block_rows
                sib_at = own_at + HALF * experts * block_rows
                part_own[j, d] = parts[own_at : own_at + block_rows]
                part_out[j, d] = parts[sib_at : sib_at + block_rows]
            y_copy(j).start()

    def add_pairs():
        for j in (1, 3, 2, 0):
            y_copy(j).wait_recv()
            part_own[j] = part_own[j] + part_in[j]
            if j % 2:
                pair_sum[j] = part_own[j].astype(jnp.bfloat16)
                pair_copy(j).start()

    def pass_pairs():
        for j in (1, 3):
            pair_copy(j).wait_recv()
        beyond = part_own[2] + pair_in[3].astype(jnp.float32)
        pair_sum[2] = beyond.astype(jnp.bfloat16)
        pair_copy(2).start()

    def finish_sums():
        pair_copy(2).wait_recv()
        total = part_own[0] + pair_in[1].astype(jnp.float32) + pair_in[2].astype(jnp.float32)
        final[...] = total.astype(jnp.bfloat16)
        own_sums.start()
        for d in range(1, experts):
            ret_copy(d).start()

    def gather(x, to_q, to_rope, to_new):
        want = flipped(branch % tok, x, 3)
        at = 0
        for t in range(tok):
            at = jnp.where(slot_ref[t] == want, t, at)
        to_q[x] = q_own[at]
        to_rope[x] = rope_own[at]
        lat = new_lat.shape[2]
        fresh_rope = new_rope[at].astype(jnp.float32)
        to_new[x, 0:2, pl.ds(0, lat)] = new_lat[at]
        to_new[x, 0:2, pl.ds(lat, lanes)] = jnp.concatenate(
            [fresh_rope, fresh_rope], axis=1
        ).astype(jnp.bfloat16)

    def send_query(x, at, where):
        gather(x, q_send, rope_send, new_send)
        for copy in query_copies(x, at, where):
            copy.start()

    def await_query(at):
        for copy in query_copies(0, at, beside):
            copy.wait_recv()

    low = lax.broadcasted_iota(jnp.int32, (packed_len, lanes), 1) < lanes // 2

    def pack_rope():
        krope_load.wait()
        groups = kraw.shape[1] // lanes
        depth = kraw.shape[0] // 2
        wide = jnp.concatenate(
            [
                jnp.concatenate(
                    [
                        kraw[pl.ds(h * depth, depth), pl.ds(g * lanes, lanes)]
                        for g in range(groups)
                    ],
                    axis=0,
                )
                for h in range(2)
            ],
            axis=1,
        )
        at = lax.broadcasted_iota(jnp.int32, (packed_len, groups * depth), 0)
        of = lax.broadcasted_iota(jnp.int32, (packed_len, groups * depth), 1)
        want = (at % (2 * groups)) // 2 * depth + at // (2 * groups)
        spreading = jnp.where(of == want, 1.0, 0.0).astype(jnp.bfloat16)
        both = lax.dot_general(spreading, wide, NN, preferred_element_type=jnp.float32)
        first = both[:, :lanes]
        later = both[:, lanes:]
        even = lax.broadcasted_iota(jnp.int32, (packed_len, lanes), 0) % 2 == 0
        left = jnp.where(even, first, pltpu.roll(first, lanes // 2, 1))
        right = jnp.where(even, pltpu.roll(later, lanes // 2, 1), later)
        kpack[0, 0] = jnp.where(low, left, right).astype(jnp.bfloat16)

    def spread(s, h):
        values = kpack[s, h].astype(jnp.float32)
        turned = pltpu.roll(values, lanes // 2, 1)
        kdup[s, h, pl.ds(0, packed_len)] = jnp.where(low, values, turned).astype(jnp.bfloat16)
        kdup[s, h, pl.ds(packed_len, packed_len)] = jnp.where(low, turned, values).astype(
            jnp.bfloat16
        )

    second = lax.broadcasted_iota(jnp.int32, (rows, 1), 0) >= heads
    half_of_row = lax.broadcasted_iota(jnp.int32, (rows, lanes), 0) % 2
    half_of_lane = lax.broadcasted_iota(jnp.int32, (rows, lanes), 1) // (lanes // 2)
    same_half = half_of_row == half_of_lane

    def make_picking():
        at = lax.broadcasted_iota(jnp.int32, picking.shape, 0)
        of = lax.broadcasted_iota(jnp.int32, picking.shape, 1)
        want = 2 * ((at % heads) // 2) + at // heads
        picking[...] = jnp.where(of == want, 1.0, 0.0).astype(jnp.bfloat16)

    def attend(i, s):
        q = q_in[i]
        spaced = lax.dot_general(picking[...], rope_in[i], NN, preferred_element_type=jnp.float32)
        qr = jnp.where(same_half, spaced, 0.0).astype(jnp.bfloat16)
        fresh = new_in[i]
        lat = q.shape[1]

        def score(k, kr):
            return lax.dot_general(q, k, NT, preferred_element_type=jnp.float32) + lax.dot_general(
                qr, kr, NT, preferred_element_type=jnp.float32
            )

        own = score(fresh[:, :lat], fresh[:, lat:])
        own0 = own[:, 0:1]
        own1 = jnp.where(second, own[:, 1:2], -1e30)
        s0 = score(keys[s, 0], kdup[s, 0])
        s1 = score(keys[s, 1], kdup[s, 1])
        top = jnp.maximum(jnp.max(s0, axis=1, keepdims=True), jnp.max(s1, axis=1, keepdims=True))
        top = jnp.maximum(top, jnp.maximum(own0, own1))
        p0 = jnp.exp((s0 - top) * softmax_scale)
        p1 = jnp.exp((s1 - top) * softmax_scale)
        w0 = jnp.exp((own0 - top) * softmax_scale)
        w1 = jnp.where(second, jnp.exp((own1 - top) * softmax_scale), 0.0)
        total = jnp.sum(p0, axis=1, keepdims=True) + jnp.sum(p1, axis=1, keepdims=True) + w0 + w1
        summed = lax.dot_general(
            p0.astype(jnp.bfloat16), keys[s, 0], NN, preferred_element_type=jnp.float32
        ) + lax.dot_general(
            p1.astype(jnp.bfloat16), keys[s, 1], NN, preferred_element_type=jnp.float32
        )
        entries = fresh[:, :lat].astype(jnp.float32)
        summed = summed + w0 * entries[0:1] + w1 * entries[1:2]
        return (summed / total).astype(jnp.bfloat16)

    def local_copy(x):
        return pltpu.make_async_copy(result.at[x], answers.at[x], local_sem.at[x])

    def both_tokens(x, s, ahead):
        def body(i, carry):
            remote_turn = i if not ahead else 1 - i
            at = x + remote_turn

            @pl.when(remote_turn == 1)
            def _():
                await_query(at)

            result[at] = attend(at, s)

            @pl.when(remote_turn == 1)
            def _():
                answer_copy(at, at, peer(1)).start()

            @pl.when(remote_turn == 0)
            def _():
                local_copy(at).start()

            return carry

        lax.fori_loop(0, 2, body, 0)

    def await_sibling_rope(s):
        sib_rope(s).wait_recv()
        spread(s, 1)

    def await_sibling(s):
        for c in range(CHUNKS):
            sib_copy(s, c).wait_recv()

    def settle():
        for c in range(CHUNKS):
            flow_copy(0, c).wait_send()
            for t in range(2):
                sib_copy(t, c).wait_send()
        flow_rope(0).wait_send()
        for t in range(2):
            sib_rope(t).wait_send()
        for x in (1, 3, 7):
            for copy in query_copies(x, x, peer(1)):
                copy.wait_send()
        for d in range(1, experts):
            cross_copy(d).wait_send()
        for j in range(HALF):
            mixsib_copy(j).wait_send()
            y_copy(j).wait_send()
            if j:
                mix_copy(j).wait_send()
            if j % 2:
                pair_copy(j).wait_send()
        local_copy(0).wait()
        answer_copy(1, 1, peer(1)).wait_send()
        answer_copy(1, 1, peer(1)).wait_recv()

        @pl.when(inner)
        def _():
            for c in range(CHUNKS):
                flow_copy(1, c).wait_send()
                flow_copy(2, c).wait_send()
                sib_copy(3, c).wait_send()
            flow_rope(1).wait_send()
            flow_rope(2).wait_send()
            sib_rope(3).wait_send()
            for copy in query_copies(5, 5, peer(1)):
                copy.wait_send()

    def own_cache(c):
        sib_copy(0, c).start()
        flow_copy(0, c).start()

    def own_over_middle(chunks):
        @pl.when(inner)
        def _():
            for c in chunks:
                flow_copy(1, c).start()

    first = max(1, CHUNKS // 8)
    own_over_middle(range(first))
    for c in range(first):
        own_cache(c)
    make_blocks()
    own_over_middle(range(first, CHUNKS // 2))
    for c in range(first, 2 * first):
        own_cache(c)
    for copy in weight_loads:
        copy.start()
    for copy in [q_load, rope_load, lat_load, new_load]:
        copy.wait()
    send_query(1, 1, peer(1))
    pack_rope()
    sib_rope(0).start()
    flow_rope(0).start()

    @pl.when(inner)
    def _():
        flow_rope(1).start()

    make_picking()
    spread(0, 0)
    gather(0, q_in, rope_in, new_in)
    mix_blocks()
    for c in range(2 * first, CHUNKS // 2):
        own_cache(c)

    pass_blocks()
    for c in range(CHUNKS // 2, CHUNKS):
        own_cache(c)

    @pl.when(outer)
    def _():
        send_query(5, 9, peer(3))
        send_query(4, 8, peer(2))

    send_query(3, 3, peer(1))
    send_query(7, 7, peer(1))

    @pl.when(inner)
    def _():
        send_query(5, 5, peer(1))
        gather(4, q_in, rope_in, new_in)

    for x in (2, 6):
        gather(x, q_in, rope_in, new_in)
    key_load.wait()
    await_sibling_rope(0)
    await_sibling(0)
    both_tokens(0, 0, False)
    share_blocks()

    def arrived(c):
        flow_copy(0, c).wait_recv()
        sib_copy(1, c).start()

        @pl.when(inner)
        def _():
            flow_copy(2, c).start()

    for c in range(CHUNKS // 4):
        arrived(c)
    flow_rope(0).wait_recv()
    sib_rope(1).start()

    @pl.when(inner)
    def _():
        flow_rope(2).start()

    feed_forward()
    for c in range(CHUNKS // 4, CHUNKS // 2):
        arrived(c)
    spread(1, 0)
    await_sibling_rope(1)
    add_pairs()

    @pl.when(inner)
    def _():
        def body(i, carry):
            @pl.when(i < 4)
            def _():
                for k in range(CHUNKS // 8):
                    arrived(CHUNKS // 2 + i * (CHUNKS // 8) + k)

            @pl.when(i == 3)
            def _():
                for c in range(CHUNKS // 2, CHUNKS):
                    flow_copy(1, c).start()

            for k in range(CHUNKS // 8):
                c = i * (CHUNKS // 8) + k
                flow_copy(2, c).wait_recv()
                flow_copy(3, c).start()
                sib_copy(3, c).start()

            @pl.when(i == 1)
            def _():
                flow_rope(2).wait_recv()
                flow_rope(3).start()
                sib_rope(3).start()
                flow_rope(1).wait_recv()
                sib_rope(2).start()

            @pl.when(i == 3)
            def _():
                pass_pairs()

            @pl.when(i == 4)
            def _():
                spread(2, 0)
                await_sibling_rope(2)
                await_sibling(1)

            @pl.when((i == 5) | (i == 6))
            def _():
                at = 8 - i

                @pl.when(i == 5)
                def _():
                    await_query(3)

                result[at] = attend(at, 1)

                @pl.when(i == 5)
                def _():
                    answer_copy(3, 3, peer(1)).start()

                @pl.when(i == 6)
                def _():
                    local_copy(2).start()

            return carry

        lax.fori_loop(0, 8, body, 0)
        spread(3, 0)
        await_sibling_rope(3)
        await_sibling(3)
        both_tokens(4, 3, True)
        finish_sums()
        for c in range(CHUNKS // 2):
            flow_copy(1, c).wait_recv()
            sib_copy(2, c).start()
        settle()
        for c in range(CHUNKS // 2, CHUNKS):
            flow_copy(1, c).wait_recv()
            sib_copy(2, c).start()
        await_sibling(2)

        def last(i, carry):
            at = 9 - i

            @pl.when(i < 3)
            def _():
                await_query(at)

            result[at] = attend(at, 2)

            @pl.when(i == 0)
            def _():
                answer_copy(9, 5, peer(3)).start()

            @pl.when(i == 1)
            def _():
                answer_copy(8, 4, peer(2)).start()

            @pl.when(i == 2)
            def _():
                answer_copy(7, 7, peer(1)).start()

            @pl.when(i == 3)
            def _():
                local_copy(6).start()

            return carry

        lax.fori_loop(0, 4, last, 0)

    @pl.when(outer)
    def _():
        for c in range(CHUNKS // 2, CHUNKS):
            arrived(c)
        await_sibling(1)
        both_tokens(2, 1, False)
        pass_pairs()
        flow_rope(3).wait_recv()
        sib_rope(2).start()
        spread(2, 0)
        await_sibling_rope(2)
        for c in range(CHUNKS // 2):
            flow_copy(3, c).wait_recv()
            sib_copy(2, c).start()
        finish_sums()
        for copy in query_copies(4, 8, peer(2)):
            copy.wait_send()
        for copy in query_copies(5, 9, peer(3)):
            copy.wait_send()
        settle()
        for c in range(CHUNKS // 2, CHUNKS):
            flow_copy(3, c).wait_recv()
            sib_copy(2, c).start()
        await_sibling(2)
        both_tokens(6, 2, True)
        for x in (4, 5):
            answer_copy(x, x, peer(1)).wait_recv()

    @pl.when(inner)
    def _():
        answer_copy(5, 5, peer(1)).wait_recv()
        local_copy(4).wait()
        answer_copy(8, 4, peer(2)).wait_send()
        answer_copy(9, 5, peer(3)).wait_send()
        answer_copy(5, 5, peer(1)).wait_send()
        for c in range(CHUNKS):
            flow_copy(3, c).wait_send()
        flow_rope(3).wait_send()

    for c in range(CHUNKS):
        sib_copy(2, c).wait_send()
    sib_rope(2).wait_send()
    for x in (3, 7):
        answer_copy(x, x, peer(1)).wait_recv()
        answer_copy(x, x, peer(1)).wait_send()
    for x in (2, 6):
        local_copy(x).wait()
    for d in range(1, experts):
        ret_copy(d).wait_recv()
    own_sums.wait()
    for d in range(1, experts):
        ret_copy(d).wait_send()
    pair_copy(2).wait_send()


def attention(slots, routes, q, rope, new_lat, new_rope, keys, krope, moe, w_gate, w_up, w_down):
    tok, rows, lat = q.shape
    half_len = keys.shape[0]
    lanes = 2 * new_rope.shape[-1]
    packed_len = half_len // 2
    width = moe.shape[-1]
    experts = lax.axis_size("branch") * lax.axis_size("expert") // SHARDS
    bf = jnp.bfloat16
    vmem = pl.BlockSpec(memory_space=pltpu.VMEM)
    smem = pl.BlockSpec(memory_space=pltpu.SMEM)
    anywhere = pl.BlockSpec(memory_space=pl.ANY)
    dma = pltpu.SemaphoreType.DMA
    quad = pltpu.VMEM((HALF, experts, CAP, width), bf)
    quad_sum = pltpu.VMEM((HALF, experts, CAP, width), jnp.float32)
    block = pltpu.VMEM((experts, CAP, width), bf)
    landing = tok + 2
    return pl.pallas_call(
        attend_kernel,
        out_shape=(
            pltpu.VMEM(q.shape, bf),
            pltpu.VMEM((experts, CAP, width), bf),
        ),
        in_specs=[smem, vmem] + [anywhere] * 10,
        out_specs=(vmem, vmem),
        scratch_shapes=[
            pltpu.VMEM(q.shape, bf),
            pltpu.VMEM(rope.shape, bf),
            pltpu.VMEM(new_lat.shape, bf),
            pltpu.VMEM(new_rope.shape, bf),
            pltpu.VMEM(krope.shape, bf),
            pltpu.VMEM(moe.shape, bf),
            pltpu.VMEM(q.shape, bf),
            pltpu.VMEM(rope.shape, bf),
            pltpu.VMEM((tok, 8, lat + lanes), bf),
            pltpu.VMEM((landing,) + q.shape[1:], bf),
            pltpu.VMEM((landing,) + rope.shape[1:], bf),
            pltpu.VMEM((landing, 8, lat + lanes), bf),
            pltpu.VMEM((4, 2, half_len, lat), bf),
            pltpu.VMEM((4, 2, packed_len, lanes), bf),
            pltpu.VMEM((4, 2, half_len, lanes), bf),
            pltpu.VMEM((landing,) + q.shape[1:], bf),
            pltpu.VMEM((rows, rope.shape[1]), bf),
            pltpu.VMEM(w_gate.shape, bf),
            pltpu.VMEM(w_up.shape, bf),
            pltpu.VMEM(w_down.shape, bf),
            block,
            block,
            block,
            quad,
            quad,
            pltpu.VMEM((2 * HALF * experts * CAP, width), bf),
            quad_sum,
            quad_sum,
            quad_sum,
            quad,
            quad,
            block,
            dma((10,)),
            dma((tok,)),
            dma((1,)),
            dma((experts,)),
            dma((experts,)),
            dma((HALF,)),
            dma((HALF,)),
            dma((HALF,)),
            dma((HALF,)),
            dma((HALF,)),
            dma((HALF,)),
            dma((HALF,)),
            dma((HALF,)),
            dma((experts,)),
            dma((experts,)),
            dma((4, CHUNKS + 1)),
            dma((4, CHUNKS + 1)),
            dma((4, CHUNKS + 1)),
            dma((4, CHUNKS + 1)),
            dma((3, tok)),
            dma((3, landing)),
            dma((landing,)),
            dma((tok,)),
        ],
        compiler_params=pltpu.CompilerParams(
            collective_id=0, has_side_effects=True, vmem_limit_bytes=57 * 1024 * 1024
        ),
    )(slots, routes, q, rope, new_lat, new_rope, keys, krope, moe, w_gate, w_up, w_down)


def finish_kernel(
    slot_ref, routes_ref, gates_ref, sums_ref, source, out, moe_out, write
):
    tok = source.shape[0]
    own = lax.axis_index("branch") % tok

    def chosen(t):
        at = 0
        for x in range(tok):
            at = jnp.where(slot_ref[t] == flipped(own, x, 3), x, at)
        return at

    def writing(t):
        return pltpu.make_async_copy(source.at[chosen(t)], out.at[t], write.at[t])

    for t in range(tok):
        writing(t).start()
    experts, slots, width = sums_ref.shape
    routes = routes_ref[...]
    gates = gates_ref[...]
    row_count = routes.shape[0]
    found = hits_of(routes, experts)
    position = positions_of(found, row_count, 128)
    total = jnp.zeros((row_count, width), jnp.float32)
    for e, hit in enumerate(found):
        gate = jnp.sum(jnp.where(routes == e, gates, 0.0), axis=1, keepdims=True)
        rows = sums_ref[e].astype(jnp.float32)
        for k in range(slots):
            here = gate * jnp.where(position[:, e : e + 1] == float(k), 1.0, 0.0)
            total = total + here * rows[k : k + 1]
    for t in range(tok):
        steps = row_count // tok
        moe_out[t] = total[t * steps : (t + 1) * steps].astype(jnp.bfloat16)
    for t in range(tok):
        writing(t).wait()


def held(x):
    return pltpu.with_memory_space_constraint(x, pltpu.VMEM)


def finished(slots, routes, gates, sums, source, moe_shape):
    anywhere = pl.BlockSpec(memory_space=pl.ANY)
    vmem = pl.BlockSpec(memory_space=pltpu.VMEM)
    tok = source.shape[0]
    return pl.pallas_call(
        finish_kernel,
        out_shape=(
            jax.ShapeDtypeStruct(source.shape, source.dtype),
            jax.ShapeDtypeStruct(moe_shape, jnp.bfloat16),
        ),
        in_specs=[pl.BlockSpec(memory_space=pltpu.SMEM), vmem, vmem, vmem, vmem],
        out_specs=(anywhere, vmem),
        scratch_shapes=[
            pltpu.SemaphoreType.DMA((tok,)),
        ],
    )(slots, routes, gates, held(sums), held(source))


def on_device(
    latent_cache,
    rope_cache,
    q_latent,
    q_rope,
    new_latent,
    new_rope,
    branch_slot,
    moe_input,
    routes,
    route_gate,
    w_gate,
    w_up,
    w_down,
):
    tok_rows, step_count, head_count, lat = q_latent.shape
    lanes = 2 * new_rope.shape[-1]
    pair_rows = q_rope.shape[-1] // lanes
    rope = q_rope.reshape(tok_rows, step_count, pair_rows, lanes)
    rope = rope.transpose(0, 2, 1, 3).reshape(tok_rows, step_count * pair_rows, lanes)
    flat_routes = routes.reshape(tok_rows * step_count, -1)
    flat_gates = route_gate.reshape(tok_rows * step_count, -1)
    answers, sums = attention(
        branch_slot,
        flat_routes,
        q_latent.reshape(tok_rows, step_count * head_count, lat),
        rope,
        new_latent,
        new_rope,
        latent_cache[0],
        rope_cache[0],
        moe_input,
        w_gate[0],
        w_up[0],
        w_down[0],
    )
    attended, moe_out = finished(
        branch_slot, flat_routes, flat_gates, sums, answers, moe_input.shape
    )
    return (attended.reshape(q_latent.shape), moe_out)


def solution(mesh):
    return jax.shard_map(
        on_device,
        mesh=mesh,
        in_specs=(
            P(("group", "branch"), "expert", None),
            P(("group", "branch"), "expert", None),
            P(("group", "branch", "expert"), None, None, None),
            P(("group", "branch", "expert"), None, None),
            P(("group", "branch", "expert"), None, None),
            P(("group", "branch", "expert"), None, None),
            P(("group", "branch", "expert")),
            P(("group", "branch", "expert"), None, None),
            P(("group", "branch", "expert"), None, None),
            P(("group", "branch", "expert"), None, None),
            P(("branch", "expert"), None, None),
            P(("branch", "expert"), None, None),
            P(("branch", "expert"), None, None),
        ),
        out_specs=(
            P(("group", "branch", "expert"), None, None, None),
            P(("group", "branch", "expert"), None, None),
        ),
        check_vma=False,
    )
```

```python
import jax
import jax.numpy as jnp
from jax import lax
from jax.experimental import pallas as pl
from jax.experimental.pallas import tpu as pltpu
from jax.sharding import PartitionSpec as P

SHARDS = 8
CAP = 2
HALF = 4
CHUNKS = 8
ROPE_PART = CHUNKS

softmax_scale = 192.0 ** (-0.5)

NT = (((1,), (1,)), ((), ()))
NN = (((1,), (0,)), ((), ()))


def flipped(r, x, bits):
    out = r - r % (1 << bits)
    for j in range(bits):
        out = out + (((r // (1 << j)) + (x // (1 << j))) % 2) * (1 << j)
    return out


def hits_of(routes, experts):
    found = []
    for e in range(experts):
        found.append(jnp.sum(jnp.where(routes == e, 1.0, 0.0), axis=1, keepdims=True))
    return found


def positions_of(found, row_count, lanes):
    lane = lax.broadcasted_iota(jnp.int32, (row_count, lanes), 1)
    table = jnp.zeros((row_count, lanes), jnp.float32)
    for e, hit in enumerate(found):
        table = table + jnp.where(lane == e, hit, 0.0)
    later = lax.broadcasted_iota(jnp.int32, (row_count, row_count), 0)
    sooner = lax.broadcasted_iota(jnp.int32, (row_count, row_count), 1)
    before = jnp.where(later > sooner, 1.0, 0.0).astype(jnp.bfloat16)
    return lax.dot_general(
        before, table.astype(jnp.bfloat16), NN, preferred_element_type=jnp.float32
    )


def attend_kernel(
    slot_ref,
    routes_ref,
    q_ref,
    rope_ref,
    new_lat_ref,
    new_rope_ref,
    keys_ref,
    krope_ref,
    moe_ref,
    w_gate_ref,
    w_up_ref,
    w_down_ref,
    answers,
    sums_ref,
    q_own,
    rope_own,
    new_lat,
    new_rope,
    kraw,
    moe_own,
    q_send,
    rope_send,
    new_send,
    q_in,
    rope_in,
    new_in,
    keys,
    kpack,
    kdup,
    result,
    picking,
    w_gate,
    w_up,
    w_down,
    blocks,
    cross_in,
    mixed,
    mixed_in,
    sib_mixed,
    stacked,
    part_own,
    part_out,
    part_in,
    pair_sum,
    pair_in,
    final,
    load_sem,
    local_sem,
    own_sem,
    cross_send,
    cross_recv,
    mix_send,
    mix_recv,
    mixsib_send,
    mixsib_recv,
    y_send,
    y_recv,
    pair_send,
    pair_recv,
    ret_send,
    ret_recv,
    flow_send,
    flow_recv,
    sib_send,
    sib_recv,
    query_send,
    query_recv,
    ans_send,
    ans_recv,
):
    branch = lax.axis_index("branch")
    core = lax.axis_index("expert")
    tok = q_ref.shape[0]
    rows = q_ref.shape[1]
    half_len = keys_ref.shape[0]
    packed_len = kpack.shape[2]
    lanes = kpack.shape[3]
    heads = rows // 2
    step_rows = half_len // CHUNKS
    place_in_half = (branch // 2) % 4
    inner = ((place_in_half + 1) // 2) % 2 == 1
    outer = ((place_in_half + 1) // 2) % 2 == 0

    def place(b, c):
        return {"branch": b, "expert": c}

    sibling = place(branch, 1 - core)

    def peer(x):
        return place(flipped(branch, x, 3), core)

    middle = peer(6)
    beside = peer(2)

    experts = blocks.shape[0]
    block_rows = blocks.shape[1]
    mine = branch // HALF

    def across(d):
        return (mine + d) % experts

    def far(d):
        return place(across(d) * HALF + branch % HALF, core)

    def load(i, src, dst):
        return pltpu.make_async_copy(src, dst, load_sem.at[i])

    key_load = load(0, keys_ref, keys.at[0, 0])
    krope_load = load(1, krope_ref, kraw)
    q_load = load(2, q_ref, q_own)
    rope_load = load(3, rope_ref, rope_own)
    lat_load = load(4, new_lat_ref, new_lat)
    new_load = load(5, new_rope_ref, new_rope)
    moe_load = load(6, moe_ref, moe_own)
    weight_loads = [
        load(7, w_gate_ref, w_gate),
        load(8, w_up_ref, w_up),
        load(9, w_down_ref, w_down),
    ]
    for copy in [krope_load, q_load, rope_load, lat_load, new_load, moe_load, key_load]:
        copy.start()
    new_send[...] = jnp.zeros_like(new_send)
    new_in[...] = jnp.zeros_like(new_in)
    barrier = pltpu.get_barrier_semaphore()
    for other in (
        [sibling, middle]
        + [peer(j) for j in range(1, HALF)]
        + [far(d) for d in range(1, experts)]
    ):
        pl.semaphore_signal(
            barrier, inc=1, device_id=other, device_id_type=pl.DeviceIdType.MESH
        )
    pl.semaphore_wait(barrier, HALF + experts)

    def remote(src, dst, send, recv, where):
        return pltpu.make_async_remote_copy(
            src_ref=src,
            dst_ref=dst,
            send_sem=send,
            recv_sem=recv,
            device_id=where,
            device_id_type=pl.DeviceIdType.MESH,
        )

    def piece(c):
        return pl.ds(c * step_rows, step_rows)

    flow_from = (0, 0, 1, 3)
    flow_to = (1, 2, 3, 2)
    flow_where = (beside, middle, middle, beside)

    def flow_copy(f, c):
        src = keys.at[flow_from[f], 0, piece(c)]
        if flow_from[f] == 0:
            src = keys_ref.at[piece(c)]
        return remote(
            src,
            keys.at[flow_to[f], 0, piece(c)],
            flow_send.at[f, c],
            flow_recv.at[f, c],
            flow_where[f],
        )

    def flow_rope(f):
        return remote(
            kpack.at[flow_from[f], 0],
            kpack.at[flow_to[f], 0],
            flow_send.at[f, ROPE_PART],
            flow_recv.at[f, ROPE_PART],
            flow_where[f],
        )

    def sib_copy(s, c):
        src = keys_ref.at[piece(c)] if s == 0 else keys.at[s, 0, piece(c)]
        return remote(
            src, keys.at[s, 1, piece(c)], sib_send.at[s, c], sib_recv.at[s, c], sibling
        )

    def sib_rope(s):
        return remote(
            kpack.at[s, 0],
            kpack.at[s, 1],
            sib_send.at[s, ROPE_PART],
            sib_recv.at[s, ROPE_PART],
            sibling,
        )

    def query_copies(x, at, where):
        return [
            remote(q_send.at[x], q_in.at[at], query_send.at[0, x], query_recv.at[0, at], where),
            remote(
                rope_send.at[x], rope_in.at[at], query_send.at[1, x], query_recv.at[1, at], where
            ),
            remote(new_send.at[x], new_in.at[at], query_send.at[2, x], query_recv.at[2, at], where),
        ]

    def answer_copy(i, x, where):
        return remote(result.at[i], answers.at[x], ans_send.at[i], ans_recv.at[x], where)

    def cross_copy(d):
        return remote(
            blocks.at[across(d)], cross_in.at[d], cross_send.at[d], cross_recv.at[d], far(d)
        )

    def mix_copy(j):
        source = mixed_in.at[2] if j == 3 else mixed
        where = peer(2) if j == 2 else peer(1)
        return remote(source, mixed_in.at[j], mix_send.at[j], mix_recv.at[j], where)

    def mixsib_copy(j):
        source = mixed if j == 0 else mixed_in.at[j]
        return remote(source, sib_mixed.at[j], mixsib_send.at[j], mixsib_recv.at[j], sibling)

    def y_copy(j):
        return remote(part_out.at[j], part_in.at[j], y_send.at[j], y_recv.at[j], sibling)

    def pair_copy(j):
        where = peer(2) if j == 2 else peer(1)
        return remote(pair_sum.at[j], pair_in.at[j], pair_send.at[j], pair_recv.at[j], where)

    def ret_copy(d):
        return remote(final.at[d], sums_ref.at[mine], ret_send.at[d], ret_recv.at[d], far(experts - d))

    own_sums = pltpu.make_async_copy(final.at[0], sums_ref.at[mine], own_sem.at[0])

    def make_blocks():
        moe_load.wait()
        row_count = routes_ref.shape[0]
        found = hits_of(routes_ref[...], experts)
        position = positions_of(found, row_count, lanes)
        lane = lax.broadcasted_iota(jnp.int32, (row_count, lanes), 1)
        placing = jnp.zeros((row_count, lanes), jnp.float32)
        for e, hit in enumerate(found):
            for k in range(block_rows):
                here = hit * jnp.where(position[:, e : e + 1] == float(k), 1.0, 0.0)
                placing = placing + jnp.where(lane == e * block_rows + k, here, 0.0)
        places = max(8, experts * block_rows)
        unit = jnp.where(
            lax.broadcasted_iota(jnp.int32, (places, lanes), 0)
            == lax.broadcasted_iota(jnp.int32, (places, lanes), 1),
            1.0,
            0.0,
        ).astype(jnp.bfloat16)
        turned = lax.dot_general(
            unit, placing.astype(jnp.bfloat16), NT, preferred_element_type=jnp.float32
        ).astype(jnp.bfloat16)
        tokens = jnp.concatenate(
            [moe_own[t].astype(jnp.float32) for t in range(tok)], axis=0
        ).astype(jnp.bfloat16)
        chosen = lax.dot_general(turned, tokens, NN, preferred_element_type=jnp.float32)
        for e in range(experts):
            blocks[e] = chosen[e * block_rows : (e + 1) * block_rows].astype(jnp.bfloat16)
        for d in range(1, experts):
            cross_copy(d).start()

    def mix_blocks():
        mixed[0] = blocks[mine]
        for d in range(1, experts):
            cross_copy(d).wait_recv()
            mixed[d] = cross_in[d]
        for j in (2, 1):
            mix_copy(j).start()

    def pass_blocks():
        mixsib_copy(0).start()
        mix_copy(2).wait_recv()
        mix_copy(3).start()
        mixsib_copy(2).start()

    def share_blocks():
        for j in (1, 3):
            mix_copy(j).wait_recv()
            mixsib_copy(j).start()

    def feed_forward():
        for j in range(0, HALF):
            mixsib_copy(j).wait_recv()
        for copy in weight_loads:
            copy.wait()
        pieces = [mixed] + [mixed_in.at[j] for j in range(1, HALF)]
        pieces = pieces + [sib_mixed.at[j] for j in range(HALF)]
        rows_of = [p[d].astype(jnp.float32) for p in pieces for d in range(experts)]
        stacked[...] = jnp.concatenate(rows_of, axis=0).astype(jnp.bfloat16)
        gate = jnp.dot(stacked[...], w_gate[...], preferred_element_type=jnp.float32)
        lifted = jnp.dot(stacked[...], w_up[...], preferred_element_type=jnp.float32)
        hidden = (gate / (1.0 + jnp.exp(-gate)) * lifted).astype(jnp.bfloat16)
        parts = jnp.dot(hidden, w_down[...], preferred_element_type=jnp.float32)
        for j in range(HALF):
            for d in range(experts):
                own_at = (j * experts + d) * block_rows
                sib_at = own_at + HALF * experts * block_rows
                part_own[j, d] = parts[own_at : own_at + block_rows]
                part_out[j, d] = parts[sib_at : sib_at + block_rows]
            y_copy(j).start()

    def add_pairs():
        for j in (1, 3, 2, 0):
            y_copy(j).wait_recv()
            part_own[j] = part_own[j] + part_in[j]
            if j % 2:
                pair_sum[j] = part_own[j].astype(jnp.bfloat16)
                pair_copy(j).start()

    def pass_pairs():
        for j in (1, 3):
            pair_copy(j).wait_recv()
        beyond = part_own[2] + pair_in[3].astype(jnp.float32)
        pair_sum[2] = beyond.astype(jnp.bfloat16)
        pair_copy(2).start()

    def finish_sums():
        pair_copy(2).wait_recv()
        total = part_own[0] + pair_in[1].astype(jnp.float32) + pair_in[2].astype(jnp.float32)
        final[...] = total.astype(jnp.bfloat16)
        own_sums.start()
        for d in range(1, experts):
            ret_copy(d).start()

    def gather(x, to_q, to_rope, to_new):
        want = flipped(branch % tok, x, 3)
        at = 0
        for t in range(tok):
            at = jnp.where(slot_ref[t] == want, t, at)
        to_q[x] = q_own[at]
        to_rope[x] = rope_own[at]
        lat = new_lat.shape[2]
        fresh_rope = new_rope[at].astype(jnp.float32)
        to_new[x, 0:2, pl.ds(0, lat)] = new_lat[at]
        to_new[x, 0:2, pl.ds(lat, lanes)] = jnp.concatenate(
            [fresh_rope, fresh_rope], axis=1
        ).astype(jnp.bfloat16)

    def send_query(x, at, where):
        gather(x, q_send, rope_send, new_send)
        for copy in query_copies(x, at, where):
            copy.start()

    def await_query(at):
        for copy in query_copies(0, at, beside):
            copy.wait_recv()

    low = lax.broadcasted_iota(jnp.int32, (packed_len, lanes), 1) < lanes // 2

    def pack_rope():
        krope_load.wait()
        groups = kraw.shape[1] // lanes
        depth = kraw.shape[0] // 2
        wide = jnp.concatenate(
            [
                jnp.concatenate(
                    [
                        kraw[pl.ds(h * depth, depth), pl.ds(g * lanes, lanes)]
                        for g in range(groups)
                    ],
                    axis=0,
                )
                for h in range(2)
            ],
            axis=1,
        )
        at = lax.broadcasted_iota(jnp.int32, (packed_len, groups * depth), 0)
        of = lax.broadcasted_iota(jnp.int32, (packed_len, groups * depth), 1)
        want = (at % (2 * groups)) // 2 * depth + at // (2 * groups)
        spreading = jnp.where(of == want, 1.0, 0.0).astype(jnp.bfloat16)
        both = lax.dot_general(spreading, wide, NN, preferred_element_type=jnp.float32)
        first = both[:, :lanes]
        later = both[:, lanes:]
        even = lax.broadcasted_iota(jnp.int32, (packed_len, lanes), 0) % 2 == 0
        left = jnp.where(even, first, pltpu.roll(first, lanes // 2, 1))
        right = jnp.where(even, pltpu.roll(later, lanes // 2, 1), later)
        kpack[0, 0] = jnp.where(low, left, right).astype(jnp.bfloat16)

    def spread(s, h):
        values = kpack[s, h].astype(jnp.float32)
        turned = pltpu.roll(values, lanes // 2, 1)
        kdup[s, h, pl.ds(0, packed_len)] = jnp.where(low, values, turned).astype(jnp.bfloat16)
        kdup[s, h, pl.ds(packed_len, packed_len)] = jnp.where(low, turned, values).astype(
            jnp.bfloat16
        )

    second = lax.broadcasted_iota(jnp.int32, (rows, 1), 0) >= heads
    half_of_row = lax.broadcasted_iota(jnp.int32, (rows, lanes), 0) % 2
    half_of_lane = lax.broadcasted_iota(jnp.int32, (rows, lanes), 1) // (lanes // 2)
    same_half = half_of_row == half_of_lane

    def make_picking():
        at = lax.broadcasted_iota(jnp.int32, picking.shape, 0)
        of = lax.broadcasted_iota(jnp.int32, picking.shape, 1)
        want = 2 * ((at % heads) // 2) + at // heads
        picking[...] = jnp.where(of == want, 1.0, 0.0).astype(jnp.bfloat16)

    def attend(i, s):
        q = q_in[i]
        spaced = lax.dot_general(picking[...], rope_in[i], NN, preferred_element_type=jnp.float32)
        qr = jnp.where(same_half, spaced, 0.0).astype(jnp.bfloat16)
        fresh = new_in[i]
        lat = q.shape[1]

        def score(k, kr):
            return lax.dot_general(q, k, NT, preferred_element_type=jnp.float32) + lax.dot_general(
                qr, kr, NT, preferred_element_type=jnp.float32
            )

        own = score(fresh[:, :lat], fresh[:, lat:])
        own0 = own[:, 0:1]
        own1 = jnp.where(second, own[:, 1:2], -1e30)
        s0 = score(keys[s, 0], kdup[s, 0])
        s1 = score(keys[s, 1], kdup[s, 1])
        top = jnp.maximum(jnp.max(s0, axis=1, keepdims=True), jnp.max(s1, axis=1, keepdims=True))
        top = jnp.maximum(top, jnp.maximum(own0, own1))
        p0 = jnp.exp((s0 - top) * softmax_scale)
        p1 = jnp.exp((s1 - top) * softmax_scale)
        w0 = jnp.exp((own0 - top) * softmax_scale)
        w1 = jnp.where(second, jnp.exp((own1 - top) * softmax_scale), 0.0)
        total = jnp.sum(p0, axis=1, keepdims=True) + jnp.sum(p1, axis=1, keepdims=True) + w0 + w1
        summed = lax.dot_general(
            p0.astype(jnp.bfloat16), keys[s, 0], NN, preferred_element_type=jnp.float32
        ) + lax.dot_general(
            p1.astype(jnp.bfloat16), keys[s, 1], NN, preferred_element_type=jnp.float32
        )
        entries = fresh[:, :lat].astype(jnp.float32)
        summed = summed + w0 * entries[0:1] + w1 * entries[1:2]
        return (summed / total).astype(jnp.bfloat16)

    def local_copy(x):
        return pltpu.make_async_copy(result.at[x], answers.at[x], local_sem.at[x])

    def both_tokens(x, s, ahead):
        def body(i, carry):
            remote_turn = i if not ahead else 1 - i
            at = x + remote_turn

            @pl.when(remote_turn == 1)
            def _():
                await_query(at)

            result[at] = attend(at, s)

            @pl.when(remote_turn == 1)
            def _():
                answer_copy(at, at, peer(1)).start()

            @pl.when(remote_turn == 0)
            def _():
                local_copy(at).start()

            return carry

        lax.fori_loop(0, 2, body, 0)

    def await_sibling_rope(s):
        sib_rope(s).wait_recv()
        spread(s, 1)

    def await_sibling(s):
        for c in range(CHUNKS):
            sib_copy(s, c).wait_recv()

    def settle():
        for c in range(CHUNKS):
            flow_copy(0, c).wait_send()
            for t in range(2):
                sib_copy(t, c).wait_send()
        flow_rope(0).wait_send()
        for t in range(2):
            sib_rope(t).wait_send()
        for x in (1, 3, 7):
            for copy in query_copies(x, x, peer(1)):
                copy.wait_send()
        for d in range(1, experts):
            cross_copy(d).wait_send()
        for j in range(HALF):
            mixsib_copy(j).wait_send()
            y_copy(j).wait_send()
            if j:
                mix_copy(j).wait_send()
            if j % 2:
                pair_copy(j).wait_send()
        local_copy(0).wait()
        answer_copy(1, 1, peer(1)).wait_send()
        answer_copy(1, 1, peer(1)).wait_recv()

        @pl.when(inner)
        def _():
            for c in range(CHUNKS):
                flow_copy(1, c).wait_send()
                flow_copy(2, c).wait_send()
                sib_copy(3, c).wait_send()
            flow_rope(1).wait_send()
            flow_rope(2).wait_send()
            sib_rope(3).wait_send()
            for copy in query_copies(5, 5, peer(1)):
                copy.wait_send()

    def own_cache(c):
        sib_copy(0, c).start()
        flow_copy(0, c).start()

    def own_over_middle(chunks):
        @pl.when(inner)
        def _():
            for c in chunks:
                flow_copy(1, c).start()

    first = max(1, CHUNKS // 8)
    own_over_middle(range(first))
    for c in range(first):
        own_cache(c)
    make_blocks()
    own_over_middle(range(first, CHUNKS // 2))
    for copy in weight_loads:
        copy.start()
    for copy in [q_load, rope_load, lat_load, new_load]:
        copy.wait()
    send_query(1, 1, peer(1))
    pack_rope()
    sib_rope(0).start()
    flow_rope(0).start()

    @pl.when(inner)
    def _():
        flow_rope(1).start()

    make_picking()
    spread(0, 0)
    gather(0, q_in, rope_in, new_in)
    send_query(3, 3, peer(1))
    mix_blocks()
    for c in range(first, CHUNKS // 2):
        own_cache(c)

    pass_blocks()
    for c in range(CHUNKS // 2, CHUNKS):
        own_cache(c)

    @pl.when(outer)
    def _():
        send_query(5, 9, peer(3))
        send_query(4, 8, peer(2))

    send_query(7, 7, peer(1))

    @pl.when(inner)
    def _():
        send_query(5, 5, peer(1))
        gather(4, q_in, rope_in, new_in)

    for x in (2, 6):
        gather(x, q_in, rope_in, new_in)
    key_load.wait()
    await_sibling_rope(0)
    await_sibling(0)
    both_tokens(0, 0, False)
    share_blocks()

    def arrived(c):
        flow_copy(0, c).wait_recv()
        sib_copy(1, c).start()

        @pl.when(inner)
        def _():
            flow_copy(2, c).start()

    for c in range(CHUNKS // 4):
        arrived(c)
    flow_rope(0).wait_recv()
    sib_rope(1).start()

    @pl.when(inner)
    def _():
        flow_rope(2).start()

    feed_forward()
    for c in range(CHUNKS // 4, CHUNKS // 2):
        arrived(c)
    spread(1, 0)
    await_sibling_rope(1)
    add_pairs()

    @pl.when(inner)
    def _():
        def body(i, carry):
            @pl.when(i < 4)
            def _():
                for k in range(CHUNKS // 8):
                    arrived(CHUNKS // 2 + i * (CHUNKS // 8) + k)

            @pl.when(i == 3)
            def _():
                for c in range(CHUNKS // 2, CHUNKS):
                    flow_copy(1, c).start()

            for k in range(CHUNKS // 8):
                c = i * (CHUNKS // 8) + k
                flow_copy(2, c).wait_recv()
                flow_copy(3, c).start()
                sib_copy(3, c).start()

            @pl.when(i == 1)
            def _():
                flow_rope(2).wait_recv()
                flow_rope(3).start()
                sib_rope(3).start()
                flow_rope(1).wait_recv()
                sib_rope(2).start()

            @pl.when(i == 3)
            def _():
                pass_pairs()

            @pl.when(i == 4)
            def _():
                spread(2, 0)
                await_sibling_rope(2)
                await_sibling(1)

            @pl.when((i == 5) | (i == 6))
            def _():
                at = 8 - i

                @pl.when(i == 5)
                def _():
                    await_query(3)

                result[at] = attend(at, 1)

                @pl.when(i == 5)
                def _():
                    answer_copy(3, 3, peer(1)).start()

                @pl.when(i == 6)
                def _():
                    local_copy(2).start()

            return carry

        lax.fori_loop(0, 8, body, 0)
        spread(3, 0)
        await_sibling_rope(3)
        await_sibling(3)
        both_tokens(4, 3, True)
        finish_sums()
        for c in range(CHUNKS // 2):
            flow_copy(1, c).wait_recv()
            sib_copy(2, c).start()
        settle()
        for c in range(CHUNKS // 2, CHUNKS):
            flow_copy(1, c).wait_recv()
            sib_copy(2, c).start()
        await_sibling(2)

        def last(i, carry):
            at = 9 - i

            @pl.when(i < 3)
            def _():
                await_query(at)

            result[at] = attend(at, 2)

            @pl.when(i == 0)
            def _():
                answer_copy(9, 5, peer(3)).start()

            @pl.when(i == 1)
            def _():
                answer_copy(8, 4, peer(2)).start()

            @pl.when(i == 2)
            def _():
                answer_copy(7, 7, peer(1)).start()

            @pl.when(i == 3)
            def _():
                local_copy(6).start()

            return carry

        lax.fori_loop(0, 4, last, 0)

    @pl.when(outer)
    def _():
        for c in range(CHUNKS // 2, CHUNKS):
            arrived(c)
        await_sibling(1)
        both_tokens(2, 1, False)
        pass_pairs()
        flow_rope(3).wait_recv()
        sib_rope(2).start()
        spread(2, 0)
        await_sibling_rope(2)
        for c in range(CHUNKS // 2):
            flow_copy(3, c).wait_recv()
            sib_copy(2, c).start()
        finish_sums()
        for copy in query_copies(4, 8, peer(2)):
            copy.wait_send()
        for copy in query_copies(5, 9, peer(3)):
            copy.wait_send()
        settle()
        for c in range(CHUNKS // 2, CHUNKS):
            flow_copy(3, c).wait_recv()
            sib_copy(2, c).start()
        await_sibling(2)
        both_tokens(6, 2, True)
        for x in (4, 5):
            answer_copy(x, x, peer(1)).wait_recv()

    @pl.when(inner)
    def _():
        answer_copy(5, 5, peer(1)).wait_recv()
        local_copy(4).wait()
        answer_copy(8, 4, peer(2)).wait_send()
        answer_copy(9, 5, peer(3)).wait_send()
        answer_copy(5, 5, peer(1)).wait_send()
        for c in range(CHUNKS):
            flow_copy(3, c).wait_send()
        flow_rope(3).wait_send()

    for c in range(CHUNKS):
        sib_copy(2, c).wait_send()
    sib_rope(2).wait_send()
    for x in (3, 7):
        answer_copy(x, x, peer(1)).wait_recv()
        answer_copy(x, x, peer(1)).wait_send()
    for x in (2, 6):
        local_copy(x).wait()
    for d in range(1, experts):
        ret_copy(d).wait_recv()
    own_sums.wait()
    for d in range(1, experts):
        ret_copy(d).wait_send()
    pair_copy(2).wait_send()


def attention(slots, routes, q, rope, new_lat, new_rope, keys, krope, moe, w_gate, w_up, w_down):
    tok, rows, lat = q.shape
    half_len = keys.shape[0]
    lanes = 2 * new_rope.shape[-1]
    packed_len = half_len // 2
    width = moe.shape[-1]
    experts = lax.axis_size("branch") * lax.axis_size("expert") // SHARDS
    bf = jnp.bfloat16
    vmem = pl.BlockSpec(memory_space=pltpu.VMEM)
    smem = pl.BlockSpec(memory_space=pltpu.SMEM)
    anywhere = pl.BlockSpec(memory_space=pl.ANY)
    dma = pltpu.SemaphoreType.DMA
    quad = pltpu.VMEM((HALF, experts, CAP, width), bf)
    quad_sum = pltpu.VMEM((HALF, experts, CAP, width), jnp.float32)
    block = pltpu.VMEM((experts, CAP, width), bf)
    landing = tok + 2
    return pl.pallas_call(
        attend_kernel,
        out_shape=(
            pltpu.VMEM(q.shape, bf),
            pltpu.VMEM((experts, CAP, width), bf),
        ),
        in_specs=[smem, vmem] + [anywhere] * 10,
        out_specs=(vmem, vmem),
        scratch_shapes=[
            pltpu.VMEM(q.shape, bf),
            pltpu.VMEM(rope.shape, bf),
            pltpu.VMEM(new_lat.shape, bf),
            pltpu.VMEM(new_rope.shape, bf),
            pltpu.VMEM(krope.shape, bf),
            pltpu.VMEM(moe.shape, bf),
            pltpu.VMEM(q.shape, bf),
            pltpu.VMEM(rope.shape, bf),
            pltpu.VMEM((tok, 8, lat + lanes), bf),
            pltpu.VMEM((landing,) + q.shape[1:], bf),
            pltpu.VMEM((landing,) + rope.shape[1:], bf),
            pltpu.VMEM((landing, 8, lat + lanes), bf),
            pltpu.VMEM((4, 2, half_len, lat), bf),
            pltpu.VMEM((4, 2, packed_len, lanes), bf),
            pltpu.VMEM((4, 2, half_len, lanes), bf),
            pltpu.VMEM((landing,) + q.shape[1:], bf),
            pltpu.VMEM((rows, rope.shape[1]), bf),
            pltpu.VMEM(w_gate.shape, bf),
            pltpu.VMEM(w_up.shape, bf),
            pltpu.VMEM(w_down.shape, bf),
            block,
            block,
            block,
            quad,
            quad,
            pltpu.VMEM((2 * HALF * experts * CAP, width), bf),
            quad_sum,
            quad_sum,
            quad_sum,
            quad,
            quad,
            block,
            dma((10,)),
            dma((tok,)),
            dma((1,)),
            dma((experts,)),
            dma((experts,)),
            dma((HALF,)),
            dma((HALF,)),
            dma((HALF,)),
            dma((HALF,)),
            dma((HALF,)),
            dma((HALF,)),
            dma((HALF,)),
            dma((HALF,)),
            dma((experts,)),
            dma((experts,)),
            dma((4, CHUNKS + 1)),
            dma((4, CHUNKS + 1)),
            dma((4, CHUNKS + 1)),
            dma((4, CHUNKS + 1)),
            dma((3, tok)),
            dma((3, landing)),
            dma((landing,)),
            dma((tok,)),
        ],
        compiler_params=pltpu.CompilerParams(
            collective_id=0, has_side_effects=True, vmem_limit_bytes=57 * 1024 * 1024
        ),
    )(slots, routes, q, rope, new_lat, new_rope, keys, krope, moe, w_gate, w_up, w_down)


def finish_kernel(
    slot_ref, routes_ref, gates_ref, sums_ref, source, out, moe_out, write
):
    tok = source.shape[0]
    own = lax.axis_index("branch") % tok

    def chosen(t):
        at = 0
        for x in range(tok):
            at = jnp.where(slot_ref[t] == flipped(own, x, 3), x, at)
        return at

    def writing(t):
        return pltpu.make_async_copy(source.at[chosen(t)], out.at[t], write.at[t])

    for t in range(tok):
        writing(t).start()
    experts, slots, width = sums_ref.shape
    routes = routes_ref[...]
    gates = gates_ref[...]
    row_count = routes.shape[0]
    found = hits_of(routes, experts)
    position = positions_of(found, row_count, 128)
    total = jnp.zeros((row_count, width), jnp.float32)
    for e, hit in enumerate(found):
        gate = jnp.sum(jnp.where(routes == e, gates, 0.0), axis=1, keepdims=True)
        rows = sums_ref[e].astype(jnp.float32)
        for k in range(slots):
            here = gate * jnp.where(position[:, e : e + 1] == float(k), 1.0, 0.0)
            total = total + here * rows[k : k + 1]
    for t in range(tok):
        steps = row_count // tok
        moe_out[t] = total[t * steps : (t + 1) * steps].astype(jnp.bfloat16)
    for t in range(tok):
        writing(t).wait()


def held(x):
    return pltpu.with_memory_space_constraint(x, pltpu.VMEM)


def finished(slots, routes, gates, sums, source, moe_shape):
    anywhere = pl.BlockSpec(memory_space=pl.ANY)
    vmem = pl.BlockSpec(memory_space=pltpu.VMEM)
    tok = source.shape[0]
    return pl.pallas_call(
        finish_kernel,
        out_shape=(
            jax.ShapeDtypeStruct(source.shape, source.dtype),
            jax.ShapeDtypeStruct(moe_shape, jnp.bfloat16),
        ),
        in_specs=[pl.BlockSpec(memory_space=pltpu.SMEM), vmem, vmem, vmem, vmem],
        out_specs=(anywhere, vmem),
        scratch_shapes=[
            pltpu.SemaphoreType.DMA((tok,)),
        ],
    )(slots, routes, gates, held(sums), held(source))


def on_device(
    latent_cache,
    rope_cache,
    q_latent,
    q_rope,
    new_latent,
    new_rope,
    branch_slot,
    moe_input,
    routes,
    route_gate,
    w_gate,
    w_up,
    w_down,
):
    tok_rows, step_count, head_count, lat = q_latent.shape
    lanes = 2 * new_rope.shape[-1]
    pair_rows = q_rope.shape[-1] // lanes
    rope = q_rope.reshape(tok_rows, step_count, pair_rows, lanes)
    rope = rope.transpose(0, 2, 1, 3).reshape(tok_rows, step_count * pair_rows, lanes)
    flat_routes = routes.reshape(tok_rows * step_count, -1)
    flat_gates = route_gate.reshape(tok_rows * step_count, -1)
    answers, sums = attention(
        branch_slot,
        flat_routes,
        q_latent.reshape(tok_rows, step_count * head_count, lat),
        rope,
        new_latent,
        new_rope,
        latent_cache[0],
        rope_cache[0],
        moe_input,
        w_gate[0],
        w_up[0],
        w_down[0],
    )
    attended, moe_out = finished(
        branch_slot, flat_routes, flat_gates, sums, answers, moe_input.shape
    )
    return (attended.reshape(q_latent.shape), moe_out)


def solution(mesh):
    return jax.shard_map(
        on_device,
        mesh=mesh,
        in_specs=(
            P(("group", "branch"), "expert", None),
            P(("group", "branch"), "expert", None),
            P(("group", "branch", "expert"), None, None, None),
            P(("group", "branch", "expert"), None, None),
            P(("group", "branch", "expert"), None, None),
            P(("group", "branch", "expert"), None, None),
            P(("group", "branch", "expert")),
            P(("group", "branch", "expert"), None, None),
            P(("group", "branch", "expert"), None, None),
            P(("group", "branch", "expert"), None, None),
            P(("branch", "expert"), None, None),
            P(("branch", "expert"), None, None),
            P(("branch", "expert"), None, None),
        ),
        out_specs=(
            P(("group", "branch", "expert"), None, None, None),
            P(("group", "branch", "expert"), None, None),
        ),
        check_vma=False,
    )
```

```python
import jax
import jax.numpy as jnp
from jax import lax
from jax.experimental import pallas as pl
from jax.experimental.pallas import tpu as pltpu
from jax.sharding import PartitionSpec as P

SHARDS = 8
CAP = 2
HALF = 4
CHUNKS = 8
ROPE_PART = CHUNKS

softmax_scale = 192.0 ** (-0.5)

NT = (((1,), (1,)), ((), ()))
NN = (((1,), (0,)), ((), ()))


def flipped(r, x, bits):
    out = r - r % (1 << bits)
    for j in range(bits):
        out = out + (((r // (1 << j)) + (x // (1 << j))) % 2) * (1 << j)
    return out


def hits_of(routes, experts):
    found = []
    for e in range(experts):
        found.append(jnp.sum(jnp.where(routes == e, 1.0, 0.0), axis=1, keepdims=True))
    return found


def positions_of(found, row_count, lanes):
    lane = lax.broadcasted_iota(jnp.int32, (row_count, lanes), 1)
    table = jnp.zeros((row_count, lanes), jnp.float32)
    for e, hit in enumerate(found):
        table = table + jnp.where(lane == e, hit, 0.0)
    later = lax.broadcasted_iota(jnp.int32, (row_count, row_count), 0)
    sooner = lax.broadcasted_iota(jnp.int32, (row_count, row_count), 1)
    before = jnp.where(later > sooner, 1.0, 0.0).astype(jnp.bfloat16)
    return lax.dot_general(
        before, table.astype(jnp.bfloat16), NN, preferred_element_type=jnp.float32
    )


def attend_kernel(
    slot_ref,
    routes_ref,
    q_ref,
    rope_ref,
    new_lat_ref,
    new_rope_ref,
    keys_ref,
    krope_ref,
    moe_ref,
    w_gate_ref,
    w_up_ref,
    w_down_ref,
    answers,
    sums_ref,
    q_own,
    rope_own,
    new_lat,
    new_rope,
    kraw,
    moe_own,
    q_send,
    rope_send,
    new_send,
    q_in,
    rope_in,
    new_in,
    keys,
    kpack,
    kdup,
    result,
    picking,
    w_gate,
    w_up,
    w_down,
    blocks,
    cross_in,
    mixed,
    mixed_in,
    sib_mixed,
    stacked,
    part_own,
    part_out,
    part_in,
    pair_sum,
    pair_in,
    final,
    load_sem,
    local_sem,
    own_sem,
    cross_send,
    cross_recv,
    mix_send,
    mix_recv,
    mixsib_send,
    mixsib_recv,
    y_send,
    y_recv,
    pair_send,
    pair_recv,
    ret_send,
    ret_recv,
    flow_send,
    flow_recv,
    sib_send,
    sib_recv,
    query_send,
    query_recv,
    ans_send,
    ans_recv,
):
    branch = lax.axis_index("branch")
    core = lax.axis_index("expert")
    tok = q_ref.shape[0]
    rows = q_ref.shape[1]
    half_len = keys_ref.shape[0]
    packed_len = kpack.shape[2]
    lanes = kpack.shape[3]
    heads = rows // 2
    step_rows = half_len // CHUNKS
    place_in_half = (branch // 2) % 4
    inner = ((place_in_half + 1) // 2) % 2 == 1
    outer = ((place_in_half + 1) // 2) % 2 == 0

    def place(b, c):
        return {"branch": b, "expert": c}

    sibling = place(branch, 1 - core)

    def peer(x):
        return place(flipped(branch, x, 3), core)

    middle = peer(6)
    beside = peer(2)

    experts = blocks.shape[0]
    block_rows = blocks.shape[1]
    mine = branch // HALF

    def across(d):
        return (mine + d) % experts

    def far(d):
        return place(across(d) * HALF + branch % HALF, core)

    def load(i, src, dst):
        return pltpu.make_async_copy(src, dst, load_sem.at[i])

    key_load = load(0, keys_ref, keys.at[0, 0])
    krope_load = load(1, krope_ref, kraw)
    q_load = load(2, q_ref, q_own)
    rope_load = load(3, rope_ref, rope_own)
    lat_load = load(4, new_lat_ref, new_lat)
    new_load = load(5, new_rope_ref, new_rope)
    moe_load = load(6, moe_ref, moe_own)
    weight_loads = [
        load(7, w_gate_ref, w_gate),
        load(8, w_up_ref, w_up),
        load(9, w_down_ref, w_down),
    ]
    for copy in [krope_load, q_load, rope_load, lat_load, new_load, moe_load, key_load]:
        copy.start()
    new_send[...] = jnp.zeros_like(new_send)
    new_in[...] = jnp.zeros_like(new_in)
    barrier = pltpu.get_barrier_semaphore()
    for other in (
        [sibling, middle]
        + [peer(j) for j in range(1, HALF)]
        + [far(d) for d in range(1, experts)]
    ):
        pl.semaphore_signal(
            barrier, inc=1, device_id=other, device_id_type=pl.DeviceIdType.MESH
        )
    pl.semaphore_wait(barrier, HALF + experts)

    def remote(src, dst, send, recv, where):
        return pltpu.make_async_remote_copy(
            src_ref=src,
            dst_ref=dst,
            send_sem=send,
            recv_sem=recv,
            device_id=where,
            device_id_type=pl.DeviceIdType.MESH,
        )

    def piece(c):
        return pl.ds(c * step_rows, step_rows)

    flow_from = (0, 0, 1, 3)
    flow_to = (1, 2, 3, 2)
    flow_where = (beside, middle, middle, beside)

    def flow_copy(f, c):
        src = keys.at[flow_from[f], 0, piece(c)]
        if flow_from[f] == 0:
            src = keys_ref.at[piece(c)]
        return remote(
            src,
            keys.at[flow_to[f], 0, piece(c)],
            flow_send.at[f, c],
            flow_recv.at[f, c],
            flow_where[f],
        )

    def flow_rope(f):
        return remote(
            kpack.at[flow_from[f], 0],
            kpack.at[flow_to[f], 0],
            flow_send.at[f, ROPE_PART],
            flow_recv.at[f, ROPE_PART],
            flow_where[f],
        )

    def sib_copy(s, c):
        src = keys_ref.at[piece(c)] if s == 0 else keys.at[s, 0, piece(c)]
        return remote(
            src, keys.at[s, 1, piece(c)], sib_send.at[s, c], sib_recv.at[s, c], sibling
        )

    def sib_rope(s):
        return remote(
            kpack.at[s, 0],
            kpack.at[s, 1],
            sib_send.at[s, ROPE_PART],
            sib_recv.at[s, ROPE_PART],
            sibling,
        )

    def query_copies(x, at, where):
        return [
            remote(q_send.at[x], q_in.at[at], query_send.at[0, x], query_recv.at[0, at], where),
            remote(
                rope_send.at[x], rope_in.at[at], query_send.at[1, x], query_recv.at[1, at], where
            ),
            remote(new_send.at[x], new_in.at[at], query_send.at[2, x], query_recv.at[2, at], where),
        ]

    def answer_copy(i, x, where):
        return remote(result.at[i], answers.at[x], ans_send.at[i], ans_recv.at[x], where)

    def cross_copy(d):
        return remote(
            blocks.at[across(d)], cross_in.at[d], cross_send.at[d], cross_recv.at[d], far(d)
        )

    def mix_copy(j):
        source = mixed_in.at[2] if j == 3 else mixed
        where = peer(2) if j == 2 else peer(1)
        return remote(source, mixed_in.at[j], mix_send.at[j], mix_recv.at[j], where)

    def mixsib_copy(j):
        source = mixed if j == 0 else mixed_in.at[j]
        return remote(source, sib_mixed.at[j], mixsib_send.at[j], mixsib_recv.at[j], sibling)

    def y_copy(j):
        return remote(part_out.at[j], part_in.at[j], y_send.at[j], y_recv.at[j], sibling)

    def pair_copy(j):
        where = peer(2) if j == 2 else peer(1)
        return remote(pair_sum.at[j], pair_in.at[j], pair_send.at[j], pair_recv.at[j], where)

    def ret_copy(d):
        return remote(final.at[d], sums_ref.at[mine], ret_send.at[d], ret_recv.at[d], far(experts - d))

    own_sums = pltpu.make_async_copy(final.at[0], sums_ref.at[mine], own_sem.at[0])

    def make_blocks():
        moe_load.wait()
        row_count = routes_ref.shape[0]
        found = hits_of(routes_ref[...], experts)
        position = positions_of(found, row_count, lanes)
        lane = lax.broadcasted_iota(jnp.int32, (row_count, lanes), 1)
        placing = jnp.zeros((row_count, lanes), jnp.float32)
        for e, hit in enumerate(found):
            for k in range(block_rows):
                here = hit * jnp.where(position[:, e : e + 1] == float(k), 1.0, 0.0)
                placing = placing + jnp.where(lane == e * block_rows + k, here, 0.0)
        places = max(8, experts * block_rows)
        unit = jnp.where(
            lax.broadcasted_iota(jnp.int32, (places, lanes), 0)
            == lax.broadcasted_iota(jnp.int32, (places, lanes), 1),
            1.0,
            0.0,
        ).astype(jnp.bfloat16)
        turned = lax.dot_general(
            unit, placing.astype(jnp.bfloat16), NT, preferred_element_type=jnp.float32
        ).astype(jnp.bfloat16)
        tokens = jnp.concatenate(
            [moe_own[t].astype(jnp.float32) for t in range(tok)], axis=0
        ).astype(jnp.bfloat16)
        chosen = lax.dot_general(turned, tokens, NN, preferred_element_type=jnp.float32)
        for e in range(experts):
            blocks[e] = chosen[e * block_rows : (e + 1) * block_rows].astype(jnp.bfloat16)
        for d in range(1, experts):
            cross_copy(d).start()

    def mix_blocks():
        mixed[0] = blocks[mine]
        for d in range(1, experts):
            cross_copy(d).wait_recv()
            mixed[d] = cross_in[d]
        for j in (2, 1):
            mix_copy(j).start()

    def pass_blocks():
        mixsib_copy(0).start()
        mix_copy(2).wait_recv()
        mix_copy(3).start()
        mixsib_copy(2).start()

    def share_blocks():
        for j in (1, 3):
            mix_copy(j).wait_recv()
            mixsib_copy(j).start()

    def feed_forward():
        for j in range(0, HALF):
            mixsib_copy(j).wait_recv()
        for copy in weight_loads:
            copy.wait()
        pieces = [mixed] + [mixed_in.at[j] for j in range(1, HALF)]
        pieces = pieces + [sib_mixed.at[j] for j in range(HALF)]
        rows_of = [p[d].astype(jnp.float32) for p in pieces for d in range(experts)]
        stacked[...] = jnp.concatenate(rows_of, axis=0).astype(jnp.bfloat16)
        gate = jnp.dot(stacked[...], w_gate[...], preferred_element_type=jnp.float32)
        lifted = jnp.dot(stacked[...], w_up[...], preferred_element_type=jnp.float32)
        hidden = (gate / (1.0 + jnp.exp(-gate)) * lifted).astype(jnp.bfloat16)
        parts = jnp.dot(hidden, w_down[...], preferred_element_type=jnp.float32)
        for j in range(HALF):
            for d in range(experts):
                own_at = (j * experts + d) * block_rows
                sib_at = own_at + HALF * experts * block_rows
                part_own[j, d] = parts[own_at : own_at + block_rows]
                part_out[j, d] = parts[sib_at : sib_at + block_rows]
            y_copy(j).start()

    def add_pairs():
        for j in (1, 3, 2, 0):
            y_copy(j).wait_recv()
            part_own[j] = part_own[j] + part_in[j]
            if j % 2:
                pair_sum[j] = part_own[j].astype(jnp.bfloat16)
                pair_copy(j).start()

    def pass_pairs():
        for j in (1, 3):
            pair_copy(j).wait_recv()
        beyond = part_own[2] + pair_in[3].astype(jnp.float32)
        pair_sum[2] = beyond.astype(jnp.bfloat16)
        pair_copy(2).start()

    def finish_sums():
        pair_copy(2).wait_recv()
        total = part_own[0] + pair_in[1].astype(jnp.float32) + pair_in[2].astype(jnp.float32)
        final[...] = total.astype(jnp.bfloat16)
        own_sums.start()
        for d in range(1, experts):
            ret_copy(d).start()

    def gather(x, to_q, to_rope, to_new):
        want = flipped(branch % tok, x, 3)
        at = 0
        for t in range(tok):
            at = jnp.where(slot_ref[t] == want, t, at)
        to_q[x] = q_own[at]
        to_rope[x] = rope_own[at]
        lat = new_lat.shape[2]
        fresh_rope = new_rope[at].astype(jnp.float32)
        to_new[x, 0:2, pl.ds(0, lat)] = new_lat[at]
        to_new[x, 0:2, pl.ds(lat, lanes)] = jnp.concatenate(
            [fresh_rope, fresh_rope], axis=1
        ).astype(jnp.bfloat16)

    def send_query(x, at, where):
        gather(x, q_send, rope_send, new_send)
        for copy in query_copies(x, at, where):
            copy.start()

    def await_query(at):
        for copy in query_copies(0, at, beside):
            copy.wait_recv()

    low = lax.broadcasted_iota(jnp.int32, (packed_len, lanes), 1) < lanes // 2

    def pack_rope():
        krope_load.wait()
        groups = kraw.shape[1] // lanes
        depth = kraw.shape[0] // 2
        wide = jnp.concatenate(
            [
                jnp.concatenate(
                    [
                        kraw[pl.ds(h * depth, depth), pl.ds(g * lanes, lanes)]
                        for g in range(groups)
                    ],
                    axis=0,
                )
                for h in range(2)
            ],
            axis=1,
        )
        at = lax.broadcasted_iota(jnp.int32, (packed_len, groups * depth), 0)
        of = lax.broadcasted_iota(jnp.int32, (packed_len, groups * depth), 1)
        want = (at % (2 * groups)) // 2 * depth + at // (2 * groups)
        spreading = jnp.where(of == want, 1.0, 0.0).astype(jnp.bfloat16)
        both = lax.dot_general(spreading, wide, NN, preferred_element_type=jnp.float32)
        first = both[:, :lanes]
        later = both[:, lanes:]
        even = lax.broadcasted_iota(jnp.int32, (packed_len, lanes), 0) % 2 == 0
        left = jnp.where(even, first, pltpu.roll(first, lanes // 2, 1))
        right = jnp.where(even, pltpu.roll(later, lanes // 2, 1), later)
        kpack[0, 0] = jnp.where(low, left, right).astype(jnp.bfloat16)

    def spread(s, h):
        values = kpack[s, h].astype(jnp.float32)
        turned = pltpu.roll(values, lanes // 2, 1)
        kdup[s, h, pl.ds(0, packed_len)] = jnp.where(low, values, turned).astype(jnp.bfloat16)
        kdup[s, h, pl.ds(packed_len, packed_len)] = jnp.where(low, turned, values).astype(
            jnp.bfloat16
        )

    second = lax.broadcasted_iota(jnp.int32, (rows, 1), 0) >= heads
    half_of_row = lax.broadcasted_iota(jnp.int32, (rows, lanes), 0) % 2
    half_of_lane = lax.broadcasted_iota(jnp.int32, (rows, lanes), 1) // (lanes // 2)
    same_half = half_of_row == half_of_lane

    def make_picking():
        at = lax.broadcasted_iota(jnp.int32, picking.shape, 0)
        of = lax.broadcasted_iota(jnp.int32, picking.shape, 1)
        want = 2 * ((at % heads) // 2) + at // heads
        picking[...] = jnp.where(of == want, 1.0, 0.0).astype(jnp.bfloat16)

    def attend(i, s):
        q = q_in[i]
        spaced = lax.dot_general(picking[...], rope_in[i], NN, preferred_element_type=jnp.float32)
        qr = jnp.where(same_half, spaced, 0.0).astype(jnp.bfloat16)
        fresh = new_in[i]
        lat = q.shape[1]

        def score(k, kr):
            return lax.dot_general(q, k, NT, preferred_element_type=jnp.float32) + lax.dot_general(
                qr, kr, NT, preferred_element_type=jnp.float32
            )

        own = score(fresh[:, :lat], fresh[:, lat:])
        own0 = own[:, 0:1]
        own1 = jnp.where(second, own[:, 1:2], -1e30)
        s0 = score(keys[s, 0], kdup[s, 0])
        s1 = score(keys[s, 1], kdup[s, 1])
        top = jnp.maximum(jnp.max(s0, axis=1, keepdims=True), jnp.max(s1, axis=1, keepdims=True))
        top = jnp.maximum(top, jnp.maximum(own0, own1))
        p0 = jnp.exp((s0 - top) * softmax_scale)
        p1 = jnp.exp((s1 - top) * softmax_scale)
        w0 = jnp.exp((own0 - top) * softmax_scale)
        w1 = jnp.where(second, jnp.exp((own1 - top) * softmax_scale), 0.0)
        total = jnp.sum(p0, axis=1, keepdims=True) + jnp.sum(p1, axis=1, keepdims=True) + w0 + w1
        summed = lax.dot_general(
            p0.astype(jnp.bfloat16), keys[s, 0], NN, preferred_element_type=jnp.float32
        ) + lax.dot_general(
            p1.astype(jnp.bfloat16), keys[s, 1], NN, preferred_element_type=jnp.float32
        )
        entries = fresh[:, :lat].astype(jnp.float32)
        summed = summed + w0 * entries[0:1] + w1 * entries[1:2]
        return (summed / total).astype(jnp.bfloat16)

    def local_copy(x):
        return pltpu.make_async_copy(result.at[x], answers.at[x], local_sem.at[x])

    def both_tokens(x, s, ahead):
        def body(i, carry):
            remote_turn = i if not ahead else 1 - i
            at = x + remote_turn

            @pl.when(remote_turn == 1)
            def _():
                await_query(at)

            result[at] = attend(at, s)

            @pl.when(remote_turn == 1)
            def _():
                answer_copy(at, at, peer(1)).start()

            @pl.when(remote_turn == 0)
            def _():
                local_copy(at).start()

            return carry

        lax.fori_loop(0, 2, body, 0)

    def await_sibling_rope(s):
        sib_rope(s).wait_recv()
        spread(s, 1)

    def await_sibling(s):
        for c in range(CHUNKS):
            sib_copy(s, c).wait_recv()

    def settle():
        for c in range(CHUNKS):
            flow_copy(0, c).wait_send()
            for t in range(2):
                sib_copy(t, c).wait_send()
        flow_rope(0).wait_send()
        for t in range(2):
            sib_rope(t).wait_send()
        for x in (1, 3, 7):
            for copy in query_copies(x, x, peer(1)):
                copy.wait_send()
        for d in range(1, experts):
            cross_copy(d).wait_send()
        for j in range(HALF):
            mixsib_copy(j).wait_send()
            y_copy(j).wait_send()
            if j:
                mix_copy(j).wait_send()
            if j % 2:
                pair_copy(j).wait_send()
        local_copy(0).wait()
        answer_copy(1, 1, peer(1)).wait_send()
        answer_copy(1, 1, peer(1)).wait_recv()

        @pl.when(inner)
        def _():
            for c in range(CHUNKS):
                flow_copy(1, c).wait_send()
                flow_copy(2, c).wait_send()
                sib_copy(3, c).wait_send()
            flow_rope(1).wait_send()
            flow_rope(2).wait_send()
            sib_rope(3).wait_send()
            for copy in query_copies(5, 5, peer(1)):
                copy.wait_send()

    def own_cache(c):
        sib_copy(0, c).start()
        flow_copy(0, c).start()

    def own_over_middle(chunks):
        @pl.when(inner)
        def _():
            for c in chunks:
                flow_copy(1, c).start()

    first = max(1, CHUNKS // 8)
    own_over_middle(range(first))
    for c in range(first):
        own_cache(c)
    for copy in [q_load, rope_load, lat_load, new_load]:
        copy.wait()
    send_query(1, 1, peer(1))
    make_blocks()
    own_over_middle(range(first, CHUNKS * 3 // 4))
    for copy in weight_loads:
        copy.start()
    pack_rope()
    sib_rope(0).start()
    flow_rope(0).start()

    @pl.when(inner)
    def _():
        flow_rope(1).start()

    make_picking()
    spread(0, 0)
    gather(0, q_in, rope_in, new_in)
    send_query(3, 3, peer(1))
    mix_blocks()
    own_cache(first)

    pass_blocks()
    for c in range(first + 1, CHUNKS):
        own_cache(c)

    @pl.when(outer)
    def _():
        send_query(5, 9, peer(3))
        send_query(4, 8, peer(2))

    send_query(7, 7, peer(1))

    @pl.when(inner)
    def _():
        send_query(5, 5, peer(1))
        gather(4, q_in, rope_in, new_in)

    for x in (2, 6):
        gather(x, q_in, rope_in, new_in)
    key_load.wait()
    await_sibling_rope(0)
    await_sibling(0)
    both_tokens(0, 0, False)
    share_blocks()

    def arrived(c):
        flow_copy(0, c).wait_recv()
        sib_copy(1, c).start()

        @pl.when(inner)
        def _():
            flow_copy(2, c).start()

    for c in range(CHUNKS // 4):
        arrived(c)
    flow_rope(0).wait_recv()
    sib_rope(1).start()

    @pl.when(inner)
    def _():
        flow_rope(2).start()

    feed_forward()
    for c in range(CHUNKS // 4, CHUNKS // 2):
        arrived(c)
    spread(1, 0)
    await_sibling_rope(1)
    add_pairs()

    @pl.when(inner)
    def _():
        def body(i, carry):
            @pl.when(i < 4)
            def _():
                for k in range(CHUNKS // 8):
                    arrived(CHUNKS // 2 + i * (CHUNKS // 8) + k)

            @pl.when(i == 3)
            def _():
                for c in range(CHUNKS * 3 // 4, CHUNKS):
                    flow_copy(1, c).start()

            for k in range(CHUNKS // 8):
                c = i * (CHUNKS // 8) + k
                flow_copy(2, c).wait_recv()
                flow_copy(3, c).start()
                sib_copy(3, c).start()

            @pl.when(i == 1)
            def _():
                flow_rope(2).wait_recv()
                flow_rope(3).start()
                sib_rope(3).start()
                flow_rope(1).wait_recv()
                sib_rope(2).start()

            @pl.when(i == 3)
            def _():
                pass_pairs()

            @pl.when(i == 4)
            def _():
                spread(2, 0)
                await_sibling_rope(2)
                await_sibling(1)

            @pl.when((i == 5) | (i == 6))
            def _():
                at = 8 - i

                @pl.when(i == 5)
                def _():
                    await_query(3)

                result[at] = attend(at, 1)

                @pl.when(i == 5)
                def _():
                    answer_copy(3, 3, peer(1)).start()

                @pl.when(i == 6)
                def _():
                    local_copy(2).start()

            return carry

        lax.fori_loop(0, 8, body, 0)
        spread(3, 0)
        await_sibling_rope(3)
        await_sibling(3)
        both_tokens(4, 3, True)
        finish_sums()
        for c in range(CHUNKS // 2):
            flow_copy(1, c).wait_recv()
            sib_copy(2, c).start()
        settle()
        for c in range(CHUNKS // 2, CHUNKS):
            flow_copy(1, c).wait_recv()
            sib_copy(2, c).start()
        await_sibling(2)

        def last(i, carry):
            at = 9 - i

            @pl.when(i < 3)
            def _():
                await_query(at)

            result[at] = attend(at, 2)

            @pl.when(i == 0)
            def _():
                answer_copy(9, 5, peer(3)).start()

            @pl.when(i == 1)
            def _():
                answer_copy(8, 4, peer(2)).start()

            @pl.when(i == 2)
            def _():
                answer_copy(7, 7, peer(1)).start()

            @pl.when(i == 3)
            def _():
                local_copy(6).start()

            return carry

        lax.fori_loop(0, 4, last, 0)

    @pl.when(outer)
    def _():
        for c in range(CHUNKS // 2, CHUNKS):
            arrived(c)
        await_sibling(1)
        both_tokens(2, 1, False)
        pass_pairs()
        flow_rope(3).wait_recv()
        sib_rope(2).start()
        spread(2, 0)
        await_sibling_rope(2)
        for c in range(CHUNKS // 2):
            flow_copy(3, c).wait_recv()
            sib_copy(2, c).start()
        finish_sums()
        for copy in query_copies(4, 8, peer(2)):
            copy.wait_send()
        for copy in query_copies(5, 9, peer(3)):
            copy.wait_send()
        settle()
        for c in range(CHUNKS // 2, CHUNKS):
            flow_copy(3, c).wait_recv()
            sib_copy(2, c).start()
        await_sibling(2)
        both_tokens(6, 2, True)
        for x in (4, 5):
            answer_copy(x, x, peer(1)).wait_recv()

    @pl.when(inner)
    def _():
        answer_copy(5, 5, peer(1)).wait_recv()
        local_copy(4).wait()
        answer_copy(8, 4, peer(2)).wait_send()
        answer_copy(9, 5, peer(3)).wait_send()
        answer_copy(5, 5, peer(1)).wait_send()
        for c in range(CHUNKS):
            flow_copy(3, c).wait_send()
        flow_rope(3).wait_send()

    for c in range(CHUNKS):
        sib_copy(2, c).wait_send()
    sib_rope(2).wait_send()
    for x in (3, 7):
        answer_copy(x, x, peer(1)).wait_recv()
        answer_copy(x, x, peer(1)).wait_send()
    for x in (2, 6):
        local_copy(x).wait()
    for d in range(1, experts):
        ret_copy(d).wait_recv()
    own_sums.wait()
    for d in range(1, experts):
        ret_copy(d).wait_send()
    pair_copy(2).wait_send()


def attention(slots, routes, q, rope, new_lat, new_rope, keys, krope, moe, w_gate, w_up, w_down):
    tok, rows, lat = q.shape
    half_len = keys.shape[0]
    lanes = 2 * new_rope.shape[-1]
    packed_len = half_len // 2
    width = moe.shape[-1]
    experts = lax.axis_size("branch") * lax.axis_size("expert") // SHARDS
    bf = jnp.bfloat16
    vmem = pl.BlockSpec(memory_space=pltpu.VMEM)
    smem = pl.BlockSpec(memory_space=pltpu.SMEM)
    anywhere = pl.BlockSpec(memory_space=pl.ANY)
    dma = pltpu.SemaphoreType.DMA
    quad = pltpu.VMEM((HALF, experts, CAP, width), bf)
    quad_sum = pltpu.VMEM((HALF, experts, CAP, width), jnp.float32)
    block = pltpu.VMEM((experts, CAP, width), bf)
    landing = tok + 2
    return pl.pallas_call(
        attend_kernel,
        out_shape=(
            pltpu.VMEM(q.shape, bf),
            pltpu.VMEM((experts, CAP, width), bf),
        ),
        in_specs=[smem, vmem] + [anywhere] * 10,
        out_specs=(vmem, vmem),
        scratch_shapes=[
            pltpu.VMEM(q.shape, bf),
            pltpu.VMEM(rope.shape, bf),
            pltpu.VMEM(new_lat.shape, bf),
            pltpu.VMEM(new_rope.shape, bf),
            pltpu.VMEM(krope.shape, bf),
            pltpu.VMEM(moe.shape, bf),
            pltpu.VMEM(q.shape, bf),
            pltpu.VMEM(rope.shape, bf),
            pltpu.VMEM((tok, 8, lat + lanes), bf),
            pltpu.VMEM((landing,) + q.shape[1:], bf),
            pltpu.VMEM((landing,) + rope.shape[1:], bf),
            pltpu.VMEM((landing, 8, lat + lanes), bf),
            pltpu.VMEM((4, 2, half_len, lat), bf),
            pltpu.VMEM((4, 2, packed_len, lanes), bf),
            pltpu.VMEM((4, 2, half_len, lanes), bf),
            pltpu.VMEM((landing,) + q.shape[1:], bf),
            pltpu.VMEM((rows, rope.shape[1]), bf),
            pltpu.VMEM(w_gate.shape, bf),
            pltpu.VMEM(w_up.shape, bf),
            pltpu.VMEM(w_down.shape, bf),
            block,
            block,
            block,
            quad,
            quad,
            pltpu.VMEM((2 * HALF * experts * CAP, width), bf),
            quad_sum,
            quad_sum,
            quad_sum,
            quad,
            quad,
            block,
            dma((10,)),
            dma((tok,)),
            dma((1,)),
            dma((experts,)),
            dma((experts,)),
            dma((HALF,)),
            dma((HALF,)),
            dma((HALF,)),
            dma((HALF,)),
            dma((HALF,)),
            dma((HALF,)),
            dma((HALF,)),
            dma((HALF,)),
            dma((experts,)),
            dma((experts,)),
            dma((4, CHUNKS + 1)),
            dma((4, CHUNKS + 1)),
            dma((4, CHUNKS + 1)),
            dma((4, CHUNKS + 1)),
            dma((3, tok)),
            dma((3, landing)),
            dma((landing,)),
            dma((tok,)),
        ],
        compiler_params=pltpu.CompilerParams(
            collective_id=0, has_side_effects=True, vmem_limit_bytes=57 * 1024 * 1024
        ),
    )(slots, routes, q, rope, new_lat, new_rope, keys, krope, moe, w_gate, w_up, w_down)


def finish_kernel(
    slot_ref, routes_ref, gates_ref, sums_ref, source, out, moe_out, write
):
    tok = source.shape[0]
    own = lax.axis_index("branch") % tok

    def chosen(t):
        at = 0
        for x in range(tok):
            at = jnp.where(slot_ref[t] == flipped(own, x, 3), x, at)
        return at

    def writing(t):
        return pltpu.make_async_copy(source.at[chosen(t)], out.at[t], write.at[t])

    for t in range(tok):
        writing(t).start()
    experts, slots, width = sums_ref.shape
    routes = routes_ref[...]
    gates = gates_ref[...]
    row_count = routes.shape[0]
    found = hits_of(routes, experts)
    position = positions_of(found, row_count, 128)
    total = jnp.zeros((row_count, width), jnp.float32)
    for e, hit in enumerate(found):
        gate = jnp.sum(jnp.where(routes == e, gates, 0.0), axis=1, keepdims=True)
        rows = sums_ref[e].astype(jnp.float32)
        for k in range(slots):
            here = gate * jnp.where(position[:, e : e + 1] == float(k), 1.0, 0.0)
            total = total + here * rows[k : k + 1]
    for t in range(tok):
        steps = row_count // tok
        moe_out[t] = total[t * steps : (t + 1) * steps].astype(jnp.bfloat16)
    for t in range(tok):
        writing(t).wait()


def held(x):
    return pltpu.with_memory_space_constraint(x, pltpu.VMEM)


def finished(slots, routes, gates, sums, source, moe_shape):
    anywhere = pl.BlockSpec(memory_space=pl.ANY)
    vmem = pl.BlockSpec(memory_space=pltpu.VMEM)
    tok = source.shape[0]
    return pl.pallas_call(
        finish_kernel,
        out_shape=(
            jax.ShapeDtypeStruct(source.shape, source.dtype),
            jax.ShapeDtypeStruct(moe_shape, jnp.bfloat16),
        ),
        in_specs=[pl.BlockSpec(memory_space=pltpu.SMEM), vmem, vmem, vmem, vmem],
        out_specs=(anywhere, vmem),
        scratch_shapes=[
            pltpu.SemaphoreType.DMA((tok,)),
        ],
    )(slots, routes, gates, held(sums), held(source))


def on_device(
    latent_cache,
    rope_cache,
    q_latent,
    q_rope,
    new_latent,
    new_rope,
    branch_slot,
    moe_input,
    routes,
    route_gate,
    w_gate,
    w_up,
    w_down,
):
    tok_rows, step_count, head_count, lat = q_latent.shape
    lanes = 2 * new_rope.shape[-1]
    pair_rows = q_rope.shape[-1] // lanes
    rope = q_rope.reshape(tok_rows, step_count, pair_rows, lanes)
    rope = rope.transpose(0, 2, 1, 3).reshape(tok_rows, step_count * pair_rows, lanes)
    flat_routes = routes.reshape(tok_rows * step_count, -1)
    flat_gates = route_gate.reshape(tok_rows * step_count, -1)
    answers, sums = attention(
        branch_slot,
        flat_routes,
        q_latent.reshape(tok_rows, step_count * head_count, lat),
        rope,
        new_latent,
        new_rope,
        latent_cache[0],
        rope_cache[0],
        moe_input,
        w_gate[0],
        w_up[0],
        w_down[0],
    )
    attended, moe_out = finished(
        branch_slot, flat_routes, flat_gates, sums, answers, moe_input.shape
    )
    return (attended.reshape(q_latent.shape), moe_out)


def solution(mesh):
    return jax.shard_map(
        on_device,
        mesh=mesh,
        in_specs=(
            P(("group", "branch"), "expert", None),
            P(("group", "branch"), "expert", None),
            P(("group", "branch", "expert"), None, None, None),
            P(("group", "branch", "expert"), None, None),
            P(("group", "branch", "expert"), None, None),
            P(("group", "branch", "expert"), None, None),
            P(("group", "branch", "expert")),
            P(("group", "branch", "expert"), None, None),
            P(("group", "branch", "expert"), None, None),
            P(("group", "branch", "expert"), None, None),
            P(("branch", "expert"), None, None),
            P(("branch", "expert"), None, None),
            P(("branch", "expert"), None, None),
        ),
        out_specs=(
            P(("group", "branch", "expert"), None, None, None),
            P(("group", "branch", "expert"), None, None),
        ),
        check_vma=False,
    )
```
